256 devices in a mesh: table: 32 (over y, z), group: 8 (over x, core).
Axes of the slice: x: 4, y: 4, z: 8, core: 2. Of those that a mesh axis runs over, the one named last changes fastest.
Arguments:
- item_owner: int32 [131072, 1], P(('table', 'group')), may hold values from 0 to 31; in each aligned block of 512 rows (0 to 511, 512 to 1023, ...) at most 24 rows name the same one
- item_row: int32 [131072], P(('table', 'group')), may hold values from 0 to 2047
- lengths: int32 [256, 8], P(('table', 'group')), may hold values from 1 to 256, 512 in all within a row
- table: bfloat16 [65536, 512], P('table'), may hold values from -6 to 6
- w_in: bfloat16 [512, 2048], replicated, may hold values from -0.25 to 0.25
- w_out: bfloat16 [512, 512], replicated, may hold values from -0.25 to 0.25
- gain: float32 [512], replicated, may hold values from 0.1 to 1.9
- cotangent: bfloat16 [131072, 512], P(('table', 'group')), may hold values from -6 to 6
Outputs:
- result: bfloat16 [131072, 512], P(('table', 'group'))
- table_grad: float32 [65536, 512], P(('table', 'group'))
- w_in_grad: float32 [512, 2048], P('table', 'group')
- w_out_grad: float32 [512, 512], P('table')
- gain_grad: float32 [512], P('table')
The draws below stay inside these ranges and needn't reach their ends.
Inputs may be any that keep to these rules, and one draw needn't show every extreme that they name: `item_owner`: among the 512 items of one device, no index of table owns more than 24 items' rows, a bound that some block reaches.
All inputs are finite; a program needn't handle non-finite values.
Results may differ from the reference program's by a relative error of at most 0.008.
Values may be sent and summed in bfloat16 or wider, within the bound.
A program may use at most 128 MiB of HBM per device.

```python
import math
import jax
import jax.numpy as jnp
import numpy as np
from jax import lax

D = 512
HEADS = 8
HEAD_DIM = 64
TOK_DEV = 512
SEGS = 8
LMAX = 256
ITEM_DEV = 2048
CAP = 24
OWNERS = 32
TOKENS = 131072
ITEMS = 65536
N_TABLE = 32
N_GROUP = 8


def touch_ends(drawn, own_key, low, largest):
    place = [jax.random.randint(jax.random.fold_in(own_key, axis), (), 0, length) for axis, length in enumerate(drawn.shape)]
    widest = drawn.shape.index(max(drawn.shape))
    next_to = place[:widest] + [(place[widest] + 1) % drawn.shape[widest]] + place[widest + 1:]
    return drawn.at[tuple(place)].set(low).at[tuple(next_to)].set(largest)


def block_scale(key, shape, pieces, low, largest):
    def one(dim, shards_of):
        steps = jax.random.uniform(jax.random.fold_in(jax.random.fold_in(key, 6), dim), (shards_of,), jnp.float32, low / len(pieces), largest / len(pieces))
        return jnp.repeat(jnp.exp(steps), shape[dim] // shards_of).reshape((-1,) + (1,) * (len(shape) - dim - 1))

    factor_of = one(*pieces[0])
    for cut in pieces[1:]:
        factor_of = factor_of * one(*cut)
    return factor_of


def profile(amount, total, bound, lean):
    portions = [(1 << 20) // math.isqrt(standing ** lean) + 1 for standing in range(2, amount + 1)]
    rest, given = total - bound - (amount - 1), [1] * (amount - 1)
    while rest > 0:
        candidates = [i for i in range(amount - 1) if given[i] < bound]
        mass, remaining = sum([portions[i] for i in candidates]), rest
        for i in candidates:
            extra = min(bound - given[i], max(1, remaining * portions[i] // mass), rest)
            given[i] = given[i] + extra
            rest = rest - extra
    return np.array([bound] + given)


def uneven(stream_key, number_of, total, bound, lean):
    if number_of == 2:
        one = jax.random.randint(stream_key, (), max(1, total - bound), min(bound, total - 1) + 1)
        return jnp.stack([one, total - one])
    sizes = jnp.asarray(profile(number_of, total, bound, lean), jnp.int32)
    couples = (number_of - 1) // 2
    giver, receiver = sizes[1:1 + 2 * couples:2], sizes[2:2 + 2 * couples:2]
    room = jnp.minimum(giver - 1, bound - receiver)
    shifted = jax.random.randint(jax.random.fold_in(stream_key, 1), (couples,), 0, 1 << 20) % (room + 1)
    sizes = sizes.at[1:1 + 2 * couples:2].set(giver - shifted).at[2:2 + 2 * couples:2].set(receiver + shifted)
    return sizes[jax.random.permutation(jax.random.fold_in(stream_key, 2), number_of)]


def assign_block(own_key, own, number, rows, count, top, most, skew):
    ranking = jax.random.permutation(own_key, count)
    crowded, ordinary = shares(count, rows * top, most, skew, True), shares(count, rows * top, most, skew, False)
    places = jnp.arange(count)

    def named(sizes, turn):
        used = int((sizes > 0).sum())
        fixed = max(1, used // 4)
        passed = fixed + (places - fixed + turn * (used - fixed)) % max(1, count - fixed)
        return jnp.zeros((count,), jnp.int32).at[ranking[jnp.where(places < fixed, places, passed)]].set(jnp.asarray(sizes, jnp.int32))

    sizes = jnp.where(number % 4 == 0, named(crowded, number // 4), named(ordinary, number - number // 4 - 1))
    mixed = jax.random.permutation(jax.random.fold_in(own, 3), count)
    donor, taker = mixed[0:count // 2 * 2:2], mixed[1:count // 2 * 2:2]
    room = jnp.minimum(sizes[donor] - 1, most - sizes[taker]) // 2
    room = jnp.where((donor == ranking[0]) | (taker == ranking[0]) | (sizes[taker] == 0), 0, jnp.maximum(room, 0))
    passed = jax.random.randint(jax.random.fold_in(own, 4), (count // 2,), 0, 1 << 20) % (room + 1)
    sizes = sizes.at[donor].add(-passed).at[taker].add(passed)
    labels = jnp.searchsorted(jnp.cumsum(sizes), jnp.arange(rows * top), side="right").astype(jnp.int32)
    table = labels.reshape(top, rows).T
    table = table[jax.random.permutation(jax.random.fold_in(own, 1), rows)]
    turn = jax.random.randint(jax.random.fold_in(own, 2), (rows, 1), 0, top)
    return jnp.take_along_axis(table, (jnp.arange(top)[None, :] + turn) % top, axis=1)


def shares(amount, total, limit, skew, full):
    loads = [(1 << 20) // math.isqrt(rank ** skew) + 1 for rank in range(1, amount + 1)]
    largest = limit if full else min(limit, max(-(-total // amount), total * loads[0] // sum(loads)))
    least = 1 if total - largest >= amount - 1 else 0
    holding, surplus = [largest] + [least] * (amount - 1), total - largest - least * (amount - 1)
    while surplus > 0:
        candidates = [i for i in range(1, amount) if holding[i] < largest] or [i for i in range(1, amount) if holding[i] < limit]
        whole, budget = sum([loads[i] for i in candidates]), surplus
        for i in candidates:
            extra = min(limit - holding[i], max(1, budget * loads[i] // whole), surplus)
            holding[i] = holding[i] + extra
            surplus = surplus - extra
    return np.array(holding)


def scatter_about(own_key, extent, width, limit, split=(), kind=jnp.bfloat16):
    values = jax.random.normal(own_key, extent, jnp.float32) * width
    if len(split) > 0:
        values = block_scale(own_key, extent, split, -0.22, 0.18) * values
    return jnp.clip(values, min=-limit, max=limit).astype(kind)


def setup_inputs(seed: int = 0) -> dict:
    splits = jax.random.split(jax.random.key(seed), 9)
    item_owner_keys = jax.random.split(jax.random.fold_in(splits[0], 1), TOKENS // TOK_DEV)
    item_owner_turns = jax.random.permutation(jax.random.fold_in(splits[0], 3), TOKENS // TOK_DEV)
    item_owner = jax.vmap(lambda own, number: assign_block(jax.random.fold_in(splits[0], 2), own, number, TOK_DEV, OWNERS, 1, CAP, 2))(item_owner_keys, item_owner_turns).reshape((TOKENS, 1))
    item_row = touch_ends(jax.random.randint(splits[1], (TOKENS,), 0, ITEM_DEV), jax.random.fold_in(splits[1], 1), 0, ITEM_DEV - 1).astype(jnp.int32)
    lengths = jax.vmap(lambda own: uneven(own, SEGS, TOK_DEV, LMAX, 2))(jax.random.split(splits[2], (N_TABLE * N_GROUP))).reshape((N_TABLE * N_GROUP, SEGS)).astype(jnp.int32)
    table = scatter_about(splits[3], (ITEMS, D), 1.0, 6.0, ((0, 32),))
    w_in = scatter_about(splits[4], (D, 4 * D), D ** -0.5, 0.25)
    w_out = scatter_about(splits[5], (D, D), D ** -0.5, 0.25)
    gain = jnp.clip(1.0 + 0.18 * jax.random.normal(splits[6], (D,), jnp.float32), 0.1, 1.9)
    cotangent = scatter_about(splits[7], (TOKENS, D), 1.0, 6.0, ((0, 256),))
    return {"item_owner": item_owner, "item_row": item_row, "lengths": lengths, "table": table, "w_in": w_in, "w_out": w_out, "gain": gain, "cotangent": cotangent}


def rounded(value):
    return lax.optimization_barrier(value.astype(jnp.bfloat16))

def silu_slope(value):
    sig_val = jax.nn.sigmoid(value)
    return sig_val * (1.0 + value * (1.0 - sig_val))

def layer_block(embedded, lengths_row, w_in, w_out, gain, grad_out):
    count = embedded.shape[0]
    scale = 1.0 / math.sqrt(HEAD_DIM)
    position = jnp.arange(count, dtype=jnp.int32)
    ends = jnp.cumsum(lengths_row)
    segment = lax.optimization_barrier(jnp.sum((position[:, None] >= ends[None, :]).astype(jnp.int32), 1))
    allowed = (segment[:, None] == segment[None, :]) & (position[None, :] <= position[:, None])
    pre_act = jnp.dot(embedded, w_in, preferred_element_type=jnp.float32)
    projected = rounded(jax.nn.silu(pre_act))
    upd_part = projected[:, :D].astype(jnp.float32)
    val_heads = projected[:, D:2 * D].astype(jnp.float32).reshape(count, HEADS, HEAD_DIM)
    qry_heads = projected[:, 2 * D:3 * D].astype(jnp.float32).reshape(count, HEADS, HEAD_DIM)
    key_heads = projected[:, 3 * D:].astype(jnp.float32).reshape(count, HEADS, HEAD_DIM)
    scores = jnp.einsum('thd,shd->hts', qry_heads, key_heads) * scale
    weights = rounded(jnp.where(allowed[None], jax.nn.silu(scores), 0.0))
    weights_f = weights.astype(jnp.float32)
    attended = jnp.einsum('hts,shd->thd', weights_f, val_heads).reshape(count, D)
    centered = attended - lax.optimization_barrier(jnp.mean(attended, 1, keepdims=True))
    inv_std = lax.rsqrt(lax.optimization_barrier(jnp.mean(centered * centered, 1, keepdims=True)) + 1e-05)
    normed = centered * inv_std
    mixed = (normed * gain * upd_part).astype(jnp.bfloat16)
    result = (embedded.astype(jnp.float32) + jnp.dot(mixed, w_out, preferred_element_type=jnp.float32)).astype(jnp.bfloat16)
    grad_w_out = jnp.dot(mixed.T, grad_out, preferred_element_type=jnp.float32)
    grad_mixed = rounded(jnp.dot(grad_out, w_out.T, preferred_element_type=jnp.float32)).astype(jnp.float32)
    grad_upd = grad_mixed * normed * gain
    grad_normed = grad_mixed * gain * upd_part
    grad_gain = lax.optimization_barrier(jnp.sum(grad_mixed * normed * upd_part, 0))
    grad_att = rounded((grad_normed - lax.optimization_barrier(jnp.mean(grad_normed, 1, keepdims=True)) - normed * lax.optimization_barrier(jnp.mean(grad_normed * normed, 1, keepdims=True))) * inv_std)
    att_heads = grad_att.astype(jnp.float32).reshape(count, HEADS, HEAD_DIM)
    grad_weights = jnp.einsum('thd,shd->hts', att_heads, val_heads)
    grad_val = jnp.einsum('hts,thd->shd', weights_f, att_heads).reshape(count, D)
    grad_score = rounded(jnp.where(allowed[None], grad_weights * silu_slope(scores), 0.0) * scale).astype(jnp.float32)
    grad_qry = jnp.einsum('hts,shd->thd', grad_score, key_heads).reshape(count, D)
    grad_key = jnp.einsum('hts,thd->shd', grad_score, qry_heads).reshape(count, D)
    grad_proj = jnp.concatenate([grad_upd, grad_val, grad_qry, grad_key], 1)
    grad_pre = (grad_proj * silu_slope(pre_act)).astype(jnp.bfloat16)
    grad_w_in = jnp.dot(embedded.T, grad_pre, preferred_element_type=jnp.float32)
    grad_emb = (grad_out.astype(jnp.float32) + jnp.dot(grad_pre, w_in.T, preferred_element_type=jnp.float32)).astype(jnp.bfloat16)
    return (result, grad_emb, grad_w_in, grad_w_out, grad_gain)

def reference(item_owner, item_row, lengths, table, w_in, w_out, gain, cotangent):
    blocks = N_TABLE * N_GROUP
    item_ids = (item_owner[:, 0] * ITEM_DEV + item_row).astype(jnp.int32)
    embedded = table[item_ids]
    emb_blocks = embedded.reshape(blocks, TOK_DEV, D)
    grad_blocks = cotangent.reshape(blocks, TOK_DEV, D)

    def step(carry, piece):
        emb_piece, lens_piece, grad_piece = piece
        result, grad_emb, grad_w_in, grad_w_out, grad_gain = layer_block(emb_piece, lens_piece, w_in, w_out, gain, grad_piece)
        return ((carry[0] + grad_w_in, carry[1] + grad_w_out, carry[2] + grad_gain), (result, grad_emb))
    start = (jnp.zeros((D, 4 * D), jnp.float32), jnp.zeros((D, D), jnp.float32), jnp.zeros((D,), jnp.float32))
    sums, outputs = lax.scan(step, start, (emb_blocks, lengths, grad_blocks))
    result = outputs[0].reshape(blocks * TOK_DEV, D)
    grad_emb = outputs[1].reshape(blocks * TOK_DEV, D)
    table_grad = jax.ops.segment_sum(grad_emb.astype(jnp.float32), item_ids, num_segments=N_TABLE * ITEM_DEV)
    return (result, table_grad, sums[0], sums[1], sums[2])
```

```python
import jax
import jax.numpy as jnp
from jax import lax
from jax.experimental import pallas as pl
from jax.experimental.pallas import tpu as pltpu
from jax.sharding import PartitionSpec as P

D = 512
HEADS = 8
F32 = jnp.float32
BF16 = jnp.bfloat16
NT = (((1,), (1,)), ((), ()))
TN = (((0,), (0,)), ((), ()))
NN = (((1,), (0,)), ((), ()))


def dot(a, b, dims=NN):
    return lax.dot_general(a, b, dims, preferred_element_type=F32)


def half_lanes(x, half):
    lane = lax.broadcasted_iota(jnp.int32, x.shape, 1)
    keep = (lane < 64) if half == 0 else (lane >= 64)
    return jnp.where(keep, x, jnp.zeros_like(x))


def layer_kernel(
    len_ref, emb_ref, w_in_ref, w_out_ref, gain_ref, cot_ref,
    res_ref, gemb_ref, gwin_ref, gwout_ref, ggain_ref,
    slope_s, proj_s, w_s, d_s, mask_s, att_s, gatt_s, gpre_s, mixed_s, gacc_s,
):
    ends = []
    total = jnp.int32(0)
    for k in range(8):
        total = total + len_ref[0, k]
        ends.append(total)
    for r in range(4):
        pos = 128 * r + lax.broadcasted_iota(jnp.int32, (128, 128), 0)
        first = jnp.zeros((128, 128), jnp.int32)
        for e in ends:
            first = jnp.where(pos >= e, e, first)
        for c in range(4):
            col = 128 * c + lax.broadcasted_iota(jnp.int32, (128, 128), 1)
            ok = (col >= first) & (col <= pos)
            mask_s[pl.ds(128 * r, 128), pl.ds(128 * c, 128)] = jnp.where(ok, 1.0, 0.0)

    def project(c, carry):
        cols = pl.ds(pl.multiple_of(c * 256, 256), 256)
        for r in range(2):
            rows = pl.ds(256 * r, 256)
            pre = dot(emb_ref[rows, :], w_in_ref[:, cols])
            sig = 0.5 + 0.5 * jnp.tanh(0.5 * pre)
            act = pre * sig
            proj_s[rows, cols] = act.astype(BF16)
            slope_s[rows, cols] = sig + act * (1.0 - sig)
        return carry

    lax.fori_loop(0, 8, project, 0)

    def forward(p, carry):
        off = pl.multiple_of(p * 128, 128)
        for r in range(2):
            rows = pl.ds(256 * r, 256)
            ncol = 256 * (r + 1)
            cols = pl.ds(0, ncol)
            key = proj_s[cols, pl.ds(1536 + off, 128)]
            val = proj_s[cols, pl.ds(512 + off, 128)]
            qry = proj_s[rows, pl.ds(1024 + off, 128)] * jnp.asarray(0.0625, BF16)
            mask = mask_s[rows, cols]
            acc = None
            for half in range(2):
                h = dot(half_lanes(qry, half), key, NT)
                t = jnp.tanh(h)
                um = (1.0 + t) * mask
                w = h * um
                d_s[2 * p + half, rows, cols] = um + w * (1.0 - t)
                wb = w.astype(BF16)
                w_s[2 * p + half, rows, cols] = wb
                part = dot(wb, half_lanes(val, half))
                acc = part if acc is None else acc + part
            att_s[rows, pl.ds(off, 128)] = acc
        return carry

    lax.fori_loop(0, 4, forward, 0)

    ggain_ref[...] = jnp.zeros_like(ggain_ref)

    def middle(r, carry):
        rows = pl.ds(pl.multiple_of(r * 128, 128), 128)
        att = att_s[rows, :]
        cen = att - jnp.mean(att, 1, keepdims=True)
        inv = lax.rsqrt(jnp.mean(cen * cen, 1, keepdims=True) + 1e-05)
        normed = cen * inv
        gain = gain_ref[...]
        upd = proj_s[rows, pl.ds(0, 512)].astype(F32)
        cot = cot_ref[rows, :]
        mixed = (normed * gain * upd).astype(BF16)
        mixed_s[rows, :] = mixed
        out = dot(mixed, w_out_ref[...])
        res_ref[rows, :] = (emb_ref[rows, :].astype(F32) + out).astype(BF16)
        gmix = dot(cot, w_out_ref[...], NT).astype(BF16).astype(F32)
        gn = gmix * normed
        gpre_s[rows, pl.ds(0, 512)] = (gn * gain * slope_s[rows, pl.ds(0, 512)]).astype(BF16)
        ggain_ref[...] += jnp.sum(gn * upd, 0, keepdims=True)
        gnorm = gmix * gain * upd
        m1 = jnp.mean(gnorm, 1, keepdims=True)
        m2 = jnp.mean(gnorm * normed, 1, keepdims=True)
        gatt_s[rows, :] = ((gnorm - m1 - normed * m2) * inv).astype(BF16)
        return carry

    lax.fori_loop(0, 4, middle, 0)

    def backward(p, carry):
        off = pl.multiple_of(p * 128, 128)
        for r in range(2):
            rows = pl.ds(256 * r, 256)
            ncol = 256 * (r + 1)
            cols = pl.ds(0, ncol)
            key = proj_s[cols, pl.ds(1536 + off, 128)] * jnp.asarray(0.0625, BF16)
            val = proj_s[cols, pl.ds(512 + off, 128)]
            qry = proj_s[rows, pl.ds(1024 + off, 128)] * jnp.asarray(0.0625, BF16)
            gat = gatt_s[rows, pl.ds(off, 128)]
            gq = gk = gv = None
            for half in range(2):
                gath = half_lanes(gat, half)
                gw = dot(gath, val, NT)
                gs = (gw * d_s[2 * p + half, rows, cols]).astype(BF16)
                a = dot(gs, half_lanes(key, half))
                b = dot(gs, half_lanes(qry, half), TN)
                c = dot(w_s[2 * p + half, rows, cols], gath, TN)
                gq = a if gq is None else gq + a
                gk = b if gk is None else gk + b
                gv = c if gv is None else gv + c
            qcols = pl.ds(1024 + off, 128)
            gpre_s[rows, qcols] = (gq * slope_s[rows, qcols]).astype(BF16)
            if r == 0:
                gacc_s[0, pl.ds(0, 256), :] = gk
                gacc_s[1, pl.ds(0, 256), :] = gv
            else:
                for n, g in ((0, gk), (1, gv)):
                    dst = pl.ds((1536 if n == 0 else 512) + off, 128)
                    top = g[:256] + gacc_s[n]
                    gpre_s[pl.ds(0, 256), dst] = (top * slope_s[pl.ds(0, 256), dst]).astype(BF16)
                    gpre_s[pl.ds(256, 256), dst] = (g[256:] * slope_s[pl.ds(256, 256), dst]).astype(BF16)
        return carry

    lax.fori_loop(0, 4, backward, 0)

    def back_emb(r, carry):
        rows = pl.ds(pl.multiple_of(r * 256, 256), 256)
        for c in range(2):
            cols = pl.ds(256 * c, 256)
            g = dot(gpre_s[rows, :], w_in_ref[cols, :], NT)
            gemb_ref[rows, cols] = (cot_ref[rows, cols].astype(F32) + g).astype(BF16)
        return carry

    lax.fori_loop(0, 2, back_emb, 0)

    def back_w(c, carry):
        cols = pl.ds(pl.multiple_of(c * 256, 256), 256)
        gwin_ref[:, cols] = dot(emb_ref[...], gpre_s[:, cols], TN).astype(BF16)
        return carry

    lax.fori_loop(0, 8, back_w, 0)
    row = lax.broadcasted_iota(jnp.int32, (512, 512), 1)
    source = ((row >> 1) & 31) * 16 + (row >> 6) * 2 + (row & 1)
    order = jnp.where(lax.broadcasted_iota(jnp.int32, (512, 512), 0) == source, 1.0, 0.0).astype(BF16)
    mixed = dot(mixed_s[...], order).astype(BF16)
    gwout_ref[...] = dot(mixed, cot_ref[...], TN).astype(BF16)


def layer(lengths, emb, w_in, w_out, gain, cot):
    vm = pl.BlockSpec(memory_space=pltpu.VMEM)
    return pl.pallas_call(
        layer_kernel,
        name="layer",
        out_shape=(
            jax.ShapeDtypeStruct((512, 512), BF16),
            jax.ShapeDtypeStruct((512, 512), BF16),
            jax.ShapeDtypeStruct((512, 2048), BF16),
            jax.ShapeDtypeStruct((512, 512), BF16),
            jax.ShapeDtypeStruct((1, 512), F32),
        ),
        in_specs=[pl.BlockSpec(memory_space=pltpu.SMEM)] + [vm] * 5,
        out_specs=[vm] * 5,
        scratch_shapes=[
            pltpu.VMEM((512, 2048), F32),
            pltpu.VMEM((512, 2048), BF16),
            pltpu.VMEM((8, 512, 512), BF16),
            pltpu.VMEM((8, 512, 512), F32),
            pltpu.VMEM((512, 512), F32),
            pltpu.VMEM((512, 512), F32),
            pltpu.VMEM((512, 512), BF16),
            pltpu.VMEM((512, 2048), BF16),
            pltpu.VMEM((512, 512), BF16),
            pltpu.VMEM((2, 256, 128), F32),
        ],
        compiler_params=pltpu.CompilerParams(vmem_limit_bytes=60 * 2**20),
    )(lengths, emb, w_in, w_out, gain, cot)


MESH = pl.DeviceIdType.MESH
NY, NZ, NX = 4, 8, 4
NT_DEV = NY * NZ
TOK = 512


def at_offset(t, k, sign):
    y, z = lax.div(t, NZ), lax.rem(t, NZ)
    dy, dz = lax.div(k, NZ), lax.rem(k, NZ)
    yy = lax.rem(y + sign * dy + NY, NY)
    zz = lax.rem(z + sign * dz + NZ, NZ)
    return yy * NZ + zz


def wait_all(ref, sem):
    pltpu.make_async_copy(ref, ref, sem).wait()


def send(src, dst, send_sem, recv_sem, to):
    pltpu.make_async_remote_copy(
        src_ref=src, dst_ref=dst, send_sem=send_sem, recv_sem=recv_sem,
        device_id=to, device_id_type=MESH,
    ).start()


def iota(shape, axis):
    return lax.broadcasted_iota(jnp.int32, shape, axis)


def hot(cond):
    return jnp.where(cond, 1.0, 0.0).astype(BF16)


def fetch_kernel(
    own_ref, row_ref, table_ref, emb_ref, pa_ref, pb_ref, ids_ref,
    req, got, onehot, sbuf, rbuf, rsend, rrecv, dsend, drecv,
):
    t, g = lax.axis_index("table"), lax.axis_index("group")
    barrier = pltpu.get_barrier_semaphore()

    @pl.loop(1, NT_DEV)
    def _(k):
        pl.semaphore_signal(barrier, inc=1, device_id=(at_offset(t, k, 1), g), device_id_type=MESH)

    own = own_ref[...]
    y, z = lax.div(t, NZ), lax.rem(t, NZ)
    rel = ((lax.shift_right_logical(own, 3) - y) & (NY - 1)) * NZ + (((own & (NZ - 1)) - z) & (NZ - 1))
    is_rel = rel == iota((NT_DEV, TOK), 0)
    owners = hot(is_rel)
    before = dot(owners, hot(iota((TOK, TOK), 0) < iota((TOK, TOK), 1)))
    rank = jnp.sum(jnp.where(is_rel, before, 0.0), 0, keepdims=True).astype(jnp.int32)
    slot_a = jnp.where(rank < 16, rel * 16 + rank, -1)
    slot_b = jnp.where(rank >= 16, rel * 8 + rank - 16, -1)
    idx = row_ref[...] + 1
    ranks = hot(rank == iota((128, TOK), 0))
    high = jnp.where(is_rel, lax.shift_right_logical(idx, 6).astype(F32), 0.0).astype(BF16)
    low = jnp.where(is_rel, (idx & 63).astype(F32), 0.0).astype(BF16)
    wanted = dot(high, ranks, NT) * 64.0 + dot(low, ranks, NT)
    req[...] = wanted.astype(jnp.int32).reshape(NT_DEV, 1, 128)
    got[0] = req[0]

    pl.semaphore_wait(barrier, NT_DEV - 1)

    @pl.loop(1, NT_DEV)
    def _(i):
        k = NT_DEV - i
        send(req.at[k], got.at[k], rsend, rrecv.at[lax.div(k, NZ)], (at_offset(t, k, 1), g))

    pa_ref[...] = hot(slot_a == iota((TOK, TOK), 0))
    pb_ref[...] = hot(slot_b == iota((TOK // 2, TOK), 0))

    for b in (2, 3, 1, 0):
        first = 1 if b == 0 else 0
        wait_all(got.at[pl.ds(NZ * b + first, NZ - first)], rrecv.at[b])
        names = jnp.transpose(got[NZ * b : NZ * (b + 1), 0, :].astype(F32))
        col = jnp.concatenate(
            [names[0:16, j : j + 1] for j in range(NZ)]
            + [names[16:24, j : j + 1] for j in range(NZ)], 0
        ).astype(jnp.int32)
        for c in range(4):
            onehot[:, 512 * c : 512 * (c + 1)] = hot(col == 512 * c + 1 + iota((24 * NZ, 512), 1))
        rows = dot(onehot[...], table_ref[...])
        first16 = rows[: 16 * NZ].reshape(NZ, 16, D)
        last8 = rows[16 * NZ :].reshape(NZ, 8, D)
        folded = jnp.concatenate([last8[:, :, : D // 2], last8[:, :, D // 2 :]], 1)
        message = jnp.concatenate([first16, folded], 2).astype(BF16)
        sbuf[NZ * b : NZ * (b + 1)] = message
        if b == 0:
            rbuf[0] = message[0]

        @pl.loop(first, NZ)
        def _(i):
            k = NZ * b + (NZ - 1 + first - i)
            send(sbuf.at[k], rbuf.at[k], dsend, drecv, (at_offset(t, k, -1), g))

    ids_ref[...] = got[...]
    wait_all(req.at[pl.ds(1, NT_DEV - 1)], rsend)
    wait_all(rbuf.at[pl.ds(1, NT_DEV - 1)], drecv)
    part_a = rbuf[:, :, :D].reshape(TOK, D)
    fold = rbuf[:, :, D:].astype(F32)
    part_b = jnp.concatenate([fold[:, :8], fold[:, 8:]], 2).reshape(TOK // 2, D).astype(BF16)
    emb_ref[...] = (dot(pa_ref[...], part_a, TN) + dot(pb_ref[...], part_b, TN)).astype(BF16)
    wait_all(sbuf.at[pl.ds(1, NT_DEV - 1)], dsend)


def fetch(own, row, table):
    vm = pl.BlockSpec(memory_space=pltpu.VMEM)
    dma = pltpu.SemaphoreType.DMA
    return pl.pallas_call(
        fetch_kernel,
        name="fetch",
        out_shape=(
            jax.ShapeDtypeStruct((TOK, D), BF16),
            jax.ShapeDtypeStruct((TOK, TOK), BF16),
            jax.ShapeDtypeStruct((TOK // 2, TOK), BF16),
            jax.ShapeDtypeStruct((NT_DEV, 1, 128), jnp.int32),
        ),
        in_specs=[vm] * 3,
        out_specs=[vm] * 4,
        scratch_shapes=[
            pltpu.VMEM((NT_DEV, 1, 128), jnp.int32),
            pltpu.VMEM((NT_DEV, 1, 128), jnp.int32),
            pltpu.VMEM((24 * NZ, 2048), BF16),
            pltpu.VMEM((NT_DEV, 16, 768), BF16),
            pltpu.VMEM((NT_DEV, 16, 768), BF16),
            dma, dma((NY,)), dma, dma,
        ],
        compiler_params=pltpu.CompilerParams(
            collective_id=1, has_side_effects=True, vmem_limit_bytes=40 * 2**20
        ),
    )(own, row, table)


def return_kernel(
    pa_ref, pb_ref, ids_ref, gemb_ref, gwin_ref, gwout_ref, ggain_ref,
    tgrad_ref, wing_ref, woutg_ref, gaing_ref,
    hot_a, hot_b, obuf, ibuf,
    tc_s, tc_r, tx_s, tx_r, tx_own,
    wc_r, oc_r, wx_s, wx_r, ox_s, ox_r, wx_own, ox_own,
    wt_s, wt_r, ot_s, ot_r, og_s, og_r, g1_r, g2_s, g2_r,
    ssem, isem, tcs, tcr, txs, txr, wcs, wcr, wxs, wxr, wts, wtr, ogs, ogr,
):
    t, g = lax.axis_index("table"), lax.axis_index("group")
    x, c = lax.div(g, 2), lax.rem(g, 2)
    other = 1 - c
    barrier = pltpu.get_barrier_semaphore()

    @pl.loop(1, NT_DEV)
    def _(k):
        pl.semaphore_signal(barrier, inc=1, device_id=(at_offset(t, k, 1), g), device_id_type=MESH)

    @pl.loop(1, 2 * NX)
    def _(k):
        pl.semaphore_signal(
            barrier, inc=1, device_id=(t, lax.rem(g + k, 2 * NX)), device_id_type=MESH
        )

    def x_of(dx):
        return lax.rem(x + dx, NX)

    gemb = gemb_ref[...]
    out_a = dot(pa_ref[...], gemb).reshape(NT_DEV, 16, D)
    out_b = dot(pb_ref[...], gemb).reshape(NT_DEV, 8, D)
    for h in range(2):
        lo = 256 * h
        folded = jnp.concatenate([out_b[:, :, lo : lo + 128], out_b[:, :, lo + 128 : lo + 256]], 1)
        obuf[h] = jnp.concatenate([out_a[:, :, lo : lo + 256], folded], 2).astype(BF16)
        ibuf[h, 0] = obuf[h, 0]

    pl.semaphore_wait(barrier, NT_DEV - 1 + 2 * NX - 1)

    for h in range(2):
        @pl.loop(1, NT_DEV)
        def _(i):
            k = NT_DEV - i
            send(obuf.at[h, k], ibuf.at[h, k], ssem.at[h], isem.at[h], (at_offset(t, k, 1), g))

    partner = (t, x * 2 + other)

    @pl.loop(0, NX)
    def _(dx):
        block = x_of(dx) * 2 + other
        send(gwin_ref.at[:, pl.ds(pl.multiple_of(block * 256, 256), 256)], wc_r.at[dx],
             wcs.at[0], wcr.at[0], partner)
        send(gwout_ref.at[pl.ds(pl.multiple_of(block * 64, 64), 64), :], oc_r.at[dx],
             wcs.at[1], wcr.at[1], partner)

    @pl.loop(1, 2 * NX)
    def _(k):
        send(ggain_ref, g1_r.at[k], wcs.at[2], wcr.at[2], (t, lax.rem(g + k, 2 * NX)))

    ids = ids_ref[:, 0, :]
    high = lax.shift_right_logical(ids, 6).astype(F32).astype(BF16)
    low = (ids & 63).astype(F32).astype(BF16)

    def spread(width, start, shift):
        lane = iota((128, NT_DEV * width), 1)
        pick = hot(iota((128, NT_DEV * width), 0) == start + (lane & (width - 1)))
        both = dot(high, pick) * 64.0 + dot(low, pick)
        mine = iota((NT_DEV, NT_DEV * width), 0) == lax.shift_right_logical(
            iota((NT_DEV, NT_DEV * width), 1), shift)
        return jnp.sum(jnp.where(mine, both, 0.0), 0, keepdims=True).astype(jnp.int32)

    name_a, name_b = spread(16, 0, 4), spread(8, 16, 3)

    @pl.loop(0, 8)
    def _(i):
        start = pl.multiple_of(i * 256, 256)
        hot_a[pl.ds(start, 256), :] = hot(name_a == start + 1 + iota((256, TOK), 0))
        hot_b[pl.ds(start, 256), :] = hot(name_b == start + 1 + iota((256, TOK // 2), 0))

    wait_all(wc_r, wcr.at[0])
    wait_all(oc_r, wcr.at[1])
    for dx in (2, 1, 3, 0):
        block = x_of(dx) * 2 + c
        w = gwin_ref[:, pl.ds(pl.multiple_of(block * 256, 256), 256)].astype(F32) + wc_r[dx].astype(F32)
        o = gwout_ref[pl.ds(pl.multiple_of(block * 64, 64), 64), :].astype(F32) + oc_r[dx].astype(F32)
        if dx:
            wx_s[dx] = w.astype(BF16)
            ox_s[dx] = o.astype(BF16)
            to = (t, x_of(dx) * 2 + c)
            send(wx_s.at[dx], wx_r.at[dx], wxs.at[0], wxr.at[0], to)
            send(ox_s.at[dx], ox_r.at[dx], wxs.at[1], wxr.at[1], to)
        else:
            wx_own[...] = w
            ox_own[...] = o

    def table_rows(h, block):
        rows = pl.ds(pl.multiple_of(block * 256, 256), 256)
        part_a = ibuf[h, :, :, :256].reshape(TOK, 256)
        fold = ibuf[h, :, :, 256:].astype(F32)
        part_b = jnp.concatenate([fold[:, :8], fold[:, 8:]], 2).reshape(TOK // 2, 256).astype(BF16)
        return dot(hot_a[rows, :], part_a) + dot(hot_b[rows, :], part_b)

    def table_send(h):
        wait_all(ibuf.at[h, pl.ds(1, NT_DEV - 1)], isem.at[h])
        for dx in (2, 1, 3, 0):
            tc_s[h, dx] = table_rows(h, x_of(dx) * 2 + other).astype(BF16)
            send(tc_s.at[h, dx], tc_r.at[h, dx], tcs.at[h, dx], tcr.at[h, dx], partner)
        for dx in (2, 1, 3, 0):
            own = table_rows(h, x_of(dx) * 2 + c)
            wait_all(tc_r.at[h, dx], tcr.at[h, dx])
            own = own + tc_r[h, dx].astype(F32)
            if dx:
                tx_s[h, dx] = own.astype(BF16)
                send(tx_s.at[h, dx], tx_r.at[h, dx], txs.at[h], txr.at[h], (t, x_of(dx) * 2 + c))
            else:
                tx_own[h] = own

    def weights_table():
        wait_all(wx_r.at[pl.ds(1, NX - 1)], wxr.at[0])
        wait_all(ox_r.at[pl.ds(1, NX - 1)], wxr.at[1])
        w = wx_own[...] + wx_r[1].astype(F32) + wx_r[2].astype(F32) + wx_r[3].astype(F32)
        o = ox_own[...] + ox_r[1].astype(F32) + ox_r[2].astype(F32) + ox_r[3].astype(F32)
        wt_s[...] = w.astype(BF16).reshape(NT_DEV, 16, 256)
        for k in range(NT_DEV):
            ot_s[k] = o[2 * k : 2 * k + 2]
        g1 = pltpu.make_async_copy(g1_r.at[pl.ds(1, 7)], g1_r.at[pl.ds(1, 7)], wcr.at[2])
        g1.wait()
        g1_r[0] = ggain_ref[...]
        g2_s[...] = jnp.sum(g1_r[...], 0)

        @pl.loop(1, NT_DEV)
        def _(k):
            to = at_offset(t, k, 1)
            send(wt_s.at[to], wt_r.at[k], wts.at[0], wtr.at[0], (to, g))
            send(ot_s.at[to], ot_r.at[k], wts.at[1], wtr.at[1], (to, g))
            send(g2_s, g2_r.at[k], wts.at[2], wtr.at[2], (to, g))

        wt_r[0] = wt_s[t]
        ot_r[0] = ot_s[t]
        g2_r[0] = g2_s[...]

    table_send(0)
    weights_table()
    table_send(1)

    rest = pl.ds(1, NT_DEV - 1)
    wait_all(wt_r.at[rest], wtr.at[0])
    wait_all(ot_r.at[rest], wtr.at[1])
    wait_all(g2_r.at[rest], wtr.at[2])
    og_s[...] = jnp.sum(ot_r[...], 0)

    @pl.loop(1, 2 * NX)
    def _(k):
        send(og_s, og_r.at[k], ogs, ogr, (t, lax.rem(g + k, 2 * NX)))

    wing_ref[...] = jnp.sum(wt_r[...].astype(F32), 0)
    total = jnp.sum(g2_r[...], 0)
    pick = jnp.where(iota((TOK, 128), 0) == 16 * t + iota((TOK, 128), 1), 1.0, 0.0)
    gaing_ref[...] = lax.dot_general(
        jnp.broadcast_to(total, (8, TOK)), pick, NN,
        precision=lax.Precision.HIGHEST, preferred_element_type=F32)[:1]

    for h in range(2):
        wait_all(tx_r.at[h, pl.ds(1, NX - 1)], txr.at[h])
        tgrad_ref[:, 256 * h : 256 * (h + 1)] = (
            tx_own[h] + tx_r[h, 1].astype(F32) + tx_r[h, 2].astype(F32) + tx_r[h, 3].astype(F32))
    og_r[0] = og_s[...]
    wait_all(og_r.at[pl.ds(1, 7)], ogr)
    woutg_ref[...] = jnp.concatenate([og_r[lax.rem(g + 2 * NX - k, 2 * NX)] for k in range(2 * NX)], 0)

    for h in range(2):
        wait_all(obuf.at[h, rest], ssem.at[h])
        wait_all(tx_s.at[h, pl.ds(1, NX - 1)], txs.at[h])
        for dx in range(NX):
            wait_all(tc_s.at[h, dx], tcs.at[h, dx])
    wait_all(wc_r, wcs.at[0])
    wait_all(oc_r, wcs.at[1])
    wait_all(g1_r.at[pl.ds(1, 7)], wcs.at[2])
    wait_all(wx_s.at[pl.ds(1, NX - 1)], wxs.at[0])
    wait_all(ox_s.at[pl.ds(1, NX - 1)], wxs.at[1])
    wait_all(wt_s.at[rest], wts.at[0])
    wait_all(ot_s.at[rest], wts.at[1])
    wait_all(g2_r.at[rest], wts.at[2])
    wait_all(og_r.at[pl.ds(1, 7)], ogs)


def give_back(pa, pb, ids, gemb, gwin, gwout, ggain):
    vm = pl.BlockSpec(memory_space=pltpu.VMEM)
    dma = pltpu.SemaphoreType.DMA
    return pl.pallas_call(
        return_kernel,
        name="give_back",
        out_shape=(
            jax.ShapeDtypeStruct((256, D), F32),
            jax.ShapeDtypeStruct((16, 256), F32),
            jax.ShapeDtypeStruct((16, D), F32),
            jax.ShapeDtypeStruct((1, 128), F32),
        ),
        in_specs=[vm] * 7,
        out_specs=[vm] * 4,
        scratch_shapes=[
            pltpu.VMEM((2048, TOK), BF16),
            pltpu.VMEM((2048, TOK // 2), BF16),
            pltpu.VMEM((2, NT_DEV, 16, 384), BF16),
            pltpu.VMEM((2, NT_DEV, 16, 384), BF16),
            pltpu.VMEM((2, NX, 256, 256), BF16),
            pltpu.VMEM((2, NX, 256, 256), BF16),
            pltpu.VMEM((2, NX, 256, 256), BF16),
            pltpu.VMEM((2, NX, 256, 256), BF16),
            pltpu.VMEM((2, 256, 256), F32),
            pltpu.VMEM((NX, 512, 256), BF16),
            pltpu.VMEM((NX, 64, 512), BF16),
            pltpu.VMEM((NX, 512, 256), BF16),
            pltpu.VMEM((NX, 512, 256), BF16),
            pltpu.VMEM((NX, 64, 512), BF16),
            pltpu.VMEM((NX, 64, 512), BF16),
            pltpu.VMEM((512, 256), F32),
            pltpu.VMEM((64, 512), F32),
            pltpu.VMEM((NT_DEV, 16, 256), BF16),
            pltpu.VMEM((NT_DEV, 16, 256), BF16),
            pltpu.VMEM((NT_DEV, 2, 512), F32),
            pltpu.VMEM((NT_DEV, 2, 512), F32),
            pltpu.VMEM((2, 512), F32),
            pltpu.VMEM((2 * NX, 2, 512), F32),
            pltpu.VMEM((2 * NX, 1, 512), F32),
            pltpu.VMEM((1, 512), F32),
            pltpu.VMEM((NT_DEV, 1, 512), F32),
            dma((2,)), dma((2,)),
            dma((2, NX)), dma((2, NX)), dma((2,)), dma((2,)),
            dma((3,)), dma((3,)), dma((2,)), dma((2,)), dma((3,)), dma((3,)), dma, dma,
        ],
        compiler_params=pltpu.CompilerParams(
            collective_id=2, has_side_effects=True, vmem_limit_bytes=60 * 2**20
        ),
    )(pa, pb, ids, gemb, gwin, gwout, ggain)


def on_device(item_owner, item_row, lengths, table, w_in, w_out, gain, cotangent):
    emb, pa, pb, ids = fetch(item_owner.reshape(1, TOK), item_row.reshape(1, TOK), table)
    result, gemb, gwin, gwout, ggain = layer(lengths, emb, w_in, w_out, gain.reshape(1, D), cotangent)
    tgrad, wing, woutg, gaing = give_back(pa, pb, ids, gemb, gwin, gwout, ggain)
    return result, tgrad, wing, woutg, gaing[0, :16]


def solution(mesh):
    return jax.shard_map(
        on_device,
        mesh=mesh,
        in_specs=(
            P(("table", "group"), None),
            P(("table", "group")),
            P(("table", "group"), None),
            P("table", None),
            P(),
            P(),
            P(),
            P(("table", "group"), None),
        ),
        out_specs=(
            P(("table", "group"), None),
            P(("table", "group"), None),
            P("table", "group"),
            P("table", None),
            P("table"),
        ),
        check_vma=False,
    )
```

```python
import types

import jax
import jax.numpy as jnp
from jax import lax
from jax.experimental import pallas as pl
from jax.experimental.pallas import tpu as pltpu
from jax.sharding import PartitionSpec as P

D = 512
TOK = 512
NY, NZ, NX = 4, 8, 4
NT_DEV = NY * NZ
CHUNKS = 2
F32 = jnp.float32
BF16 = jnp.bfloat16
I32 = jnp.int32
NT = (((1,), (1,)), ((), ()))
TN = (((0,), (0,)), ((), ()))
NN = (((1,), (0,)), ((), ()))
MESH = pl.DeviceIdType.MESH
FAR_X = (2, 1, 3)


def dot(a, b, dims=NN):
    return lax.dot_general(a, b, dims, preferred_element_type=F32)


def iota(shape, axis):
    return lax.broadcasted_iota(I32, shape, axis)


def hot(cond):
    return jnp.where(cond, 1.0, 0.0).astype(BF16)


def half_lanes(v, half):
    lane = iota(v.shape, 1)
    keep = (lane < 64) if half == 0 else (lane >= 64)
    return jnp.where(keep, v, jnp.zeros_like(v))


def at_offset(t, k, sign):
    y, z = lax.div(t, NZ), lax.rem(t, NZ)
    dy, dz = lax.div(k, NZ), lax.rem(k, NZ)
    yy = lax.rem(y + sign * dy + NY, NY)
    zz = lax.rem(z + sign * dz + NZ, NZ)
    return yy * NZ + zz


def wait_all(ref, sem):
    pltpu.make_async_copy(ref, ref, sem).wait()


def send(src, dst, send_sem, recv_sem, to):
    pltpu.make_async_remote_copy(
        src_ref=src, dst_ref=dst, send_sem=send_sem, recv_sem=recv_sem,
        device_id=to, device_id_type=MESH,
    ).start()


def block(i, size):
    return pl.ds(pl.multiple_of(i * size, size), size)


def scratch():
    vm = pltpu.VMEM
    dma = pltpu.SemaphoreType.DMA
    return dict(
        own=vm((1, TOK), I32), row=vm((1, TOK), I32), table=vm((2048, D), BF16),
        w_in=vm((D, 2048), BF16), w_out=vm((D, D), BF16), cot=vm((TOK, D), BF16),
        gain=vm((1, D), F32),
        req=vm((NT_DEV, 1, 128), I32), got=vm((NT_DEV, 1, 128), I32),
        onehot=vm((24 * NZ, 2048), BF16), sbuf=vm((NT_DEV, 16, 768), BF16),
        rbuf=vm((NT_DEV, 16, 768), BF16), pa=vm((TOK, TOK), BF16), pb=vm((TOK // 2, TOK), BF16),
        hot_a=vm((2048, TOK), BF16), hot_b=vm((2048, TOK // 2), BF16),
        emb=vm((TOK, D), BF16), emb_t=vm((D, TOK), BF16), w_in_t=vm((2048, D), BF16),
        slope=vm((TOK, 2048), F32), proj=vm((TOK, 2048), BF16), w=vm((8, TOK, TOK), BF16),
        d=vm((8, TOK, TOK), F32), mask=vm((TOK, TOK), F32), att=vm((TOK, D), F32),
        gmix=vm((TOK, D), F32), gatt=vm((TOK, D), BF16), gpre=vm((TOK, 2048), BF16),
        mixed=vm((TOK, D), BF16), gacc=vm((2, 256, 128), F32), gemb=vm((TOK, D), BF16),
        order=vm((D, D), BF16), gwout=vm((D, D), BF16), ggain=vm((1, D), F32),
        obuf=vm((CHUNKS, NT_DEV, 16, 384), BF16), ibuf=vm((CHUNKS, NT_DEV, 16, 384), BF16),
        tc_s=vm((CHUNKS, NX, 256, 256), BF16), tc_r=vm((CHUNKS, NX, 256, 256), BF16),
        tx_s=vm((CHUNKS, NX, 256, 256), BF16), tx_r=vm((CHUNKS, NX, 256, 256), BF16),
        tx_own=vm((CHUNKS, 256, 256), F32),
        wc_s=vm((NX, D, 256), BF16), wc_r=vm((NX, D, 256), BF16), oc_r=vm((NX, 64, D), BF16),
        wx_s=vm((NX, D, 256), BF16), wx_r=vm((NX, D, 256), BF16), wx_own=vm((D, 256), F32),
        ox_s=vm((NX, 64, D), BF16), ox_r=vm((NX, 64, D), BF16), ox_own=vm((64, D), F32),
        gx_r=vm((2 * NX, 1, D), F32),
        wy_s=vm((NY, 128, 256), BF16), wy_r=vm((NY, 128, 256), BF16), wy_own=vm((NY, 128, 256), F32),
        oy_s=vm((NY, 16, D), BF16), oy_r=vm((NY, 16, D), BF16), oy_own=vm((NY, 16, D), F32),
        gy_s=vm((1, D), F32), gy_r=vm((NY, 1, D), F32),
        wz_s=vm((NZ, 16, 256), BF16), wz_r=vm((NZ, 16, 256), BF16), wz_own=vm((NZ, 16, 256), F32),
        oz_s=vm((NZ, 2, D), F32), oz_r=vm((NZ, 2, D), F32),
        gz_s=vm((1, D), F32), gz_r=vm((NZ, 1, D), F32),
        og_s=vm((2, D), F32), og_r=vm((2 * NX, 2, D), F32),
        load=dma((7,)), rsend=dma, rrecv=dma((NY,)), dsend=dma, drecv=dma,
        ssem=dma((CHUNKS,)), isem=dma((CHUNKS,)),
        tcs=dma((CHUNKS, NX)), tcr=dma((CHUNKS, NX)), txs=dma((CHUNKS,)), txr=dma((CHUNKS,)),
        wcs=dma((NX,)), wcr=dma((NX,)), ocs=dma, ocr=dma, gxs=dma, gxr=dma,
        wxs=dma((2,)), wxr=dma((2,)), wys=dma((3,)), wyr=dma((3,)), wzs=dma((3,)), wzr=dma((3,)),
        ogs=dma, ogr=dma,
    )


def kernel(len_ref, own_h, row_h, table_h, w_in_h, w_out_h, gain_h, cot_h,
           res_ref, tgrad_ref, wing_ref, woutg_ref, gaing_ref, *refs):
    s = types.SimpleNamespace(**dict(zip(scratch(), refs)))
    t, g = lax.axis_index("table"), lax.axis_index("group")
    x, c = lax.div(g, 2), lax.rem(g, 2)
    other = 1 - c
    y, z = lax.div(t, NZ), lax.rem(t, NZ)
    partner = (t, x * 2 + other)
    barrier = pltpu.get_barrier_semaphore()

    loads = [
        pltpu.make_async_copy(src, dst, s.load.at[i])
        for i, (src, dst) in enumerate((
            (own_h, s.own), (row_h, s.row), (table_h, s.table), (w_out_h, s.w_out),
            (cot_h, s.cot), (w_in_h, s.w_in), (gain_h, s.gain)))
    ]
    for copy in loads:
        copy.start()

    @pl.loop(1, NT_DEV)
    def _(k):
        pl.semaphore_signal(
            barrier, inc=1, device_id=(at_offset(t, NT_DEV - k, 1), g), device_id_type=MESH)

    @pl.loop(1, 2 * NX)
    def _(k):
        pl.semaphore_signal(
            barrier, inc=1, device_id=(t, lax.rem(g + k, 2 * NX)), device_id_type=MESH)

    def x_of(dx):
        return lax.rem(x + dx, NX)

    loads[0].wait()
    loads[1].wait()
    own = s.own[...]
    rel = ((lax.shift_right_logical(own, 3) - y) & (NY - 1)) * NZ + (((own & (NZ - 1)) - z) & (NZ - 1))
    is_rel = rel == iota((NT_DEV, TOK), 0)
    before = dot(hot(is_rel), hot(iota((TOK, TOK), 0) < iota((TOK, TOK), 1)))
    rank = jnp.sum(jnp.where(is_rel, before, 0.0), 0, keepdims=True).astype(I32)
    idx = s.row[...] + 1
    ranks = hot(rank == iota((128, TOK), 0))
    high = jnp.where(is_rel, lax.shift_right_logical(idx, 6).astype(F32), 0.0).astype(BF16)
    low = jnp.where(is_rel, (idx & 63).astype(F32), 0.0).astype(BF16)
    wanted = dot(high, ranks, NT) * 64.0 + dot(low, ranks, NT)
    s.req[...] = wanted.astype(I32).reshape(NT_DEV, 1, 128)
    s.got[0] = s.req[0]

    pl.semaphore_wait(barrier, NT_DEV - 1 + 2 * NX - 1)

    @pl.loop(1, NT_DEV)
    def _(i):
        k = NT_DEV - i
        send(s.req.at[k], s.got.at[k], s.rsend, s.rrecv.at[lax.div(k, NZ)], (at_offset(t, k, 1), g))

    slot_a = jnp.where(rank < 16, rel * 16 + rank, -1)
    slot_b = jnp.where(rank >= 16, rel * 8 + rank - 16, -1)
    s.pa[...] = hot(slot_a == iota((TOK, TOK), 0))
    s.pb[...] = hot(slot_b == iota((TOK // 2, TOK), 0))
    loads[2].wait()

    for b in (3, 2, 1, 0):
        first = 1 if b == 0 else 0
        wait_all(s.got.at[pl.ds(NZ * b + first, NZ - first)], s.rrecv.at[b])
        names = jnp.transpose(s.got[NZ * b : NZ * (b + 1), 0, :].astype(F32))
        col = jnp.concatenate(
            [names[0:16, j : j + 1] for j in range(NZ)]
            + [names[16:24, j : j + 1] for j in range(NZ)], 0
        ).astype(I32)
        for q in range(4):
            s.onehot[:, 512 * q : 512 * (q + 1)] = hot(col == 512 * q + 1 + iota((24 * NZ, 512), 1))
        rows = dot(s.onehot[...], s.table[...])
        first16 = rows[: 16 * NZ].reshape(NZ, 16, D)
        last8 = rows[16 * NZ :].reshape(NZ, 8, D)
        folded = jnp.concatenate([last8[:, :, : D // 2], last8[:, :, D // 2 :]], 1)
        message = jnp.concatenate([first16, folded], 2).astype(BF16)
        s.sbuf[NZ * b : NZ * (b + 1)] = message
        if b == 0:
            s.rbuf[0] = message[0]

        @pl.loop(first, NZ)
        def _(i):
            k = NZ * b + (NZ - 1 + first - i)
            send(s.sbuf.at[k], s.rbuf.at[k], s.dsend, s.drecv, (at_offset(t, k, -1), g))

    ids = s.got[:, 0, :]
    high = lax.shift_right_logical(ids, 6).astype(F32).astype(BF16)
    low = (ids & 63).astype(F32).astype(BF16)

    def spread(width, start, shift):
        lane = iota((128, NT_DEV * width), 1)
        pick = hot(iota((128, NT_DEV * width), 0) == start + (lane & (width - 1)))
        both = dot(high, pick) * 64.0 + dot(low, pick)
        mine = iota((NT_DEV, NT_DEV * width), 0) == lax.shift_right_logical(
            iota((NT_DEV, NT_DEV * width), 1), shift)
        return jnp.sum(jnp.where(mine, both, 0.0), 0, keepdims=True).astype(I32)

    name_a, name_b = spread(16, 0, 4), spread(8, 16, 3)

    @pl.loop(0, 8)
    def _(i):
        rows = block(i, 256)
        s.hot_a[rows, :] = hot(name_a == i * 256 + 1 + iota((256, TOK), 0))
        s.hot_b[rows, :] = hot(name_b == i * 256 + 1 + iota((256, TOK // 2), 0))

    ends = []
    total = jnp.int32(0)
    for k in range(8):
        total = total + len_ref[0, k]
        ends.append(total)
    for r in range(4):
        pos = 128 * r + iota((128, 128), 0)
        start = jnp.zeros((128, 128), I32)
        for e in ends:
            start = jnp.where(pos >= e, e, start)
        for q in range(4):
            col = 128 * q + iota((128, 128), 1)
            ok = (col >= start) & (col <= pos)
            s.mask[128 * r : 128 * (r + 1), 128 * q : 128 * (q + 1)] = jnp.where(ok, 1.0, 0.0)

    loads[3].wait()
    loads[4].wait()

    @pl.loop(0, 4)
    def _(r):
        rows = block(r, 128)
        s.gmix[rows, :] = dot(s.cot[rows, :], s.w_out[...], NT).astype(BF16).astype(F32)

    lane = iota((D, D), 1)
    source = ((lane >> 1) & 31) * 16 + (lane >> 6) * 2 + (lane & 1)
    s.order[...] = hot(iota((D, D), 0) == source)
    loads[5].wait()
    loads[6].wait()

    @pl.loop(0, 8)
    def _(q):
        s.w_in_t[block(q, 256), :] = jnp.transpose(s.w_in[:, block(q, 256)])

    rest = pl.ds(1, NT_DEV - 1)
    wait_all(s.rbuf.at[rest], s.drecv)
    part_a = s.rbuf[:, :, :D].reshape(TOK, D)
    fold = s.rbuf[:, :, D:].astype(F32)
    part_b = jnp.concatenate([fold[:, :8], fold[:, 8:]], 2).reshape(TOK // 2, D).astype(BF16)
    s.emb[...] = (dot(s.pa[...], part_a, TN) + dot(s.pb[...], part_b, TN)).astype(BF16)

    @pl.loop(0, 8)
    def _(q):
        cols = block(q, 256)
        for r in range(2):
            rows = pl.ds(256 * r, 256)
            pre = dot(s.emb[rows, :], s.w_in[:, cols])
            sig = 0.5 + 0.5 * jnp.tanh(0.5 * pre)
            act = pre * sig
            s.proj[rows, cols] = act.astype(BF16)
            s.slope[rows, cols] = sig + act * (1.0 - sig)

    @pl.loop(0, 4)
    def _(p):
        off = pl.multiple_of(p * 128, 128)
        for r in range(2):
            rows = pl.ds(256 * r, 256)
            cols = pl.ds(0, 256 * (r + 1))
            key = s.proj[cols, pl.ds(1536 + off, 128)]
            val = s.proj[cols, pl.ds(512 + off, 128)]
            qry = s.proj[rows, pl.ds(1024 + off, 128)] * jnp.asarray(0.0625, BF16)
            mask = s.mask[rows, cols]
            acc = None
            for half in range(2):
                h = dot(half_lanes(qry, half), key, NT)
                th = jnp.tanh(h)
                um = (1.0 + th) * mask
                w = h * um
                s.d[2 * p + half, rows, cols] = um + w * (1.0 - th)
                wb = w.astype(BF16)
                s.w[2 * p + half, rows, cols] = wb
                part = dot(wb, half_lanes(val, half))
                acc = part if acc is None else acc + part
            s.att[rows, pl.ds(off, 128)] = acc

    s.ggain[...] = jnp.zeros_like(s.ggain)

    @pl.loop(0, 4)
    def _(r):
        rows = block(r, 128)
        att = s.att[rows, :]
        cen = att - jnp.mean(att, 1, keepdims=True)
        inv = lax.rsqrt(jnp.mean(cen * cen, 1, keepdims=True) + 1e-05)
        normed = cen * inv
        gain = s.gain[...]
        upd = s.proj[rows, pl.ds(0, 512)].astype(F32)
        s.mixed[rows, :] = (normed * gain * upd).astype(BF16)
        gmix = s.gmix[rows, :]
        gn = gmix * normed
        s.gpre[rows, pl.ds(0, 512)] = (gn * gain * s.slope[rows, pl.ds(0, 512)]).astype(BF16)
        s.ggain[...] += jnp.sum(gn * upd, 0, keepdims=True)
        gnorm = gmix * gain * upd
        m1 = jnp.mean(gnorm, 1, keepdims=True)
        m2 = jnp.mean(gnorm * normed, 1, keepdims=True)
        s.gatt[rows, :] = ((gnorm - m1 - normed * m2) * inv).astype(BF16)

    mixed = dot(s.mixed[...], s.order[...]).astype(BF16)
    s.gwout[...] = dot(mixed, s.cot[...], TN).astype(BF16)
    s.gx_r[0] = s.ggain[...]

    @pl.loop(0, NX)
    def _(dx):
        send(s.gwout.at[block(x_of(dx) * 2 + other, 64), :], s.oc_r.at[dx], s.ocs, s.ocr, partner)

    @pl.loop(1, 2 * NX)
    def _(k):
        send(s.ggain, s.gx_r.at[k], s.gxs, s.gxr, (t, lax.rem(g + k, 2 * NX)))

    @pl.loop(0, 4)
    def _(p):
        off = pl.multiple_of(p * 128, 128)
        for r in range(2):
            rows = pl.ds(256 * r, 256)
            cols = pl.ds(0, 256 * (r + 1))
            key = s.proj[cols, pl.ds(1536 + off, 128)] * jnp.asarray(0.0625, BF16)
            val = s.proj[cols, pl.ds(512 + off, 128)]
            qry = s.proj[rows, pl.ds(1024 + off, 128)] * jnp.asarray(0.0625, BF16)
            gat = s.gatt[rows, pl.ds(off, 128)]
            gq = gk = gv = None
            for half in range(2):
                gath = half_lanes(gat, half)
                gw = dot(gath, val, NT)
                gs = (gw * s.d[2 * p + half, rows, cols]).astype(BF16)
                a = dot(gs, half_lanes(key, half))
                b = dot(gs, half_lanes(qry, half), TN)
                v = dot(s.w[2 * p + half, rows, cols], gath, TN)
                gq = a if gq is None else gq + a
                gk = b if gk is None else gk + b
                gv = v if gv is None else gv + v
            qcols = pl.ds(1024 + off, 128)
            s.gpre[rows, qcols] = (gq * s.slope[rows, qcols]).astype(BF16)
            if r == 0:
                s.gacc[0] = gk
                s.gacc[1] = gv
            else:
                for n, acc in ((0, gk), (1, gv)):
                    dst = pl.ds((1536 if n == 0 else 512) + off, 128)
                    for half in range(2):
                        part = pl.ds(256 * half, 256)
                        v = acc[256 * half : 256 * (half + 1)]
                        v = v + s.gacc[n] if half == 0 else v
                        s.gpre[part, dst] = (v * s.slope[part, dst]).astype(BF16)

    @pl.loop(0, 2)
    def _(r):
        rows = block(r, 256)
        v = dot(s.gpre[rows, :], s.w_in_t[...])
        s.gemb[rows, :] = (s.cot[rows, :].astype(F32) + v).astype(BF16)

    for h in range(CHUNKS):
        cols = pl.ds(256 * h, 256)
        gemb = s.gemb[:, cols]
        out_a = dot(s.pa[...], gemb).reshape(NT_DEV, 16, 256)
        out_b = dot(s.pb[...], gemb).reshape(NT_DEV, 8, 256)
        folded = jnp.concatenate([out_b[:, :, :128], out_b[:, :, 128:]], 1)
        message = jnp.concatenate([out_a, folded], 2).astype(BF16)
        s.obuf[h] = message
        s.ibuf[h, 0] = message[0]

        @pl.loop(1, NT_DEV)
        def _(i):
            k = NT_DEV - i
            send(s.obuf.at[h, k], s.ibuf.at[h, k], s.ssem.at[h], s.isem.at[h], (at_offset(t, k, 1), g))

    wait_all(s.oc_r, s.ocr)
    for dx in FAR_X + (0,):
        o = s.gwout[block(x_of(dx) * 2 + c, 64), :].astype(F32) + s.oc_r[dx].astype(F32)
        if dx:
            s.ox_s[dx] = o.astype(BF16)
            send(s.ox_s.at[dx], s.ox_r.at[dx], s.wxs.at[1], s.wxr.at[1], (t, x_of(dx) * 2 + c))
        else:
            s.ox_own[...] = o
    s.emb_t[...] = jnp.transpose(s.emb[...])
    for dx in FAR_X + (0,):
        cols = block(x_of(dx) * 2 + other, 256)
        s.wc_s[dx] = dot(s.emb_t[...], s.gpre[:, cols]).astype(BF16)
        send(s.wc_s.at[dx], s.wc_r.at[dx], s.wcs.at[dx], s.wcr.at[dx], partner)
    for dx in FAR_X + (0,):
        w = dot(s.emb_t[...], s.gpre[:, block(x_of(dx) * 2 + c, 256)])
        wait_all(s.wc_r.at[dx], s.wcr.at[dx])
        w = w + s.wc_r[dx].astype(F32)
        if dx:
            s.wx_s[dx] = w.astype(BF16)
            send(s.wx_s.at[dx], s.wx_r.at[dx], s.wxs.at[0], s.wxr.at[0], (t, x_of(dx) * 2 + c))
        else:
            s.wx_own[...] = w

    @pl.loop(0, 4)
    def _(r):
        rows = block(r, 128)
        out = dot(s.mixed[rows, :], s.w_out[...])
        res_ref[rows, :] = (s.emb[rows, :].astype(F32) + out).astype(BF16)

    def table_rows(h, which):
        rows = block(which, 256)
        part_a = s.ibuf[h, :, :, :256].reshape(TOK, 256)
        fold = s.ibuf[h, :, :, 256:].astype(F32)
        part_b = jnp.concatenate([fold[:, :8], fold[:, 8:]], 2).reshape(TOK // 2, 256).astype(BF16)
        return dot(s.hot_a[rows, :], part_a) + dot(s.hot_b[rows, :], part_b)

    def table_send(h):
        wait_all(s.ibuf.at[h, rest], s.isem.at[h])
        for dx in FAR_X + (0,):
            s.tc_s[h, dx] = table_rows(h, x_of(dx) * 2 + other).astype(BF16)
            send(s.tc_s.at[h, dx], s.tc_r.at[h, dx], s.tcs.at[h, dx], s.tcr.at[h, dx], partner)
        for dx in FAR_X + (0,):
            own = table_rows(h, x_of(dx) * 2 + c)
            wait_all(s.tc_r.at[h, dx], s.tcr.at[h, dx])
            own = own + s.tc_r[h, dx].astype(F32)
            if dx:
                s.tx_s[h, dx] = own.astype(BF16)
                send(s.tx_s.at[h, dx], s.tx_r.at[h, dx], s.txs.at[h], s.txr.at[h],
                     (t, x_of(dx) * 2 + c))
            else:
                s.tx_own[h] = own

    rest_x, rest_y, rest_z = pl.ds(1, NX - 1), pl.ds(1, NY - 1), pl.ds(1, NZ - 1)
    rest_g = pl.ds(1, 2 * NX - 1)

    def weights_y():
        wait_all(s.wx_r.at[rest_x], s.wxr.at[0])
        wait_all(s.ox_r.at[rest_x], s.wxr.at[1])
        wait_all(s.gx_r.at[rest_g], s.gxr)
        w = s.wx_own[...] + s.wx_r[1].astype(F32) + s.wx_r[2].astype(F32) + s.wx_r[3].astype(F32)
        o = s.ox_own[...] + s.ox_r[1].astype(F32) + s.ox_r[2].astype(F32) + s.ox_r[3].astype(F32)
        s.wy_own[...] = w.reshape(NY, 128, 256)
        s.oy_own[...] = o.reshape(NY, 16, D)
        s.wy_s[...] = w.astype(BF16).reshape(NY, 128, 256)
        s.oy_s[...] = o.astype(BF16).reshape(NY, 16, D)
        s.gy_s[...] = jnp.sum(s.gx_r[...], 0)
        s.gy_r[0] = s.gy_s[...]

        @pl.loop(1, NY)
        def _(k):
            yy = lax.rem(y + k, NY)
            to = (yy * NZ + z, g)
            send(s.wy_s.at[yy], s.wy_r.at[k], s.wys.at[0], s.wyr.at[0], to)
            send(s.oy_s.at[yy], s.oy_r.at[k], s.wys.at[1], s.wyr.at[1], to)
            send(s.gy_s, s.gy_r.at[k], s.wys.at[2], s.wyr.at[2], to)

    def weights_z():
        wait_all(s.wy_r.at[rest_y], s.wyr.at[0])
        wait_all(s.oy_r.at[rest_y], s.wyr.at[1])
        wait_all(s.gy_r.at[rest_y], s.wyr.at[2])
        w = s.wy_own[y] + s.wy_r[1].astype(F32) + s.wy_r[2].astype(F32) + s.wy_r[3].astype(F32)
        o = s.oy_own[y] + s.oy_r[1].astype(F32) + s.oy_r[2].astype(F32) + s.oy_r[3].astype(F32)
        s.wz_own[...] = w.reshape(NZ, 16, 256)
        s.wz_s[...] = w.astype(BF16).reshape(NZ, 16, 256)
        for k in range(NZ):
            s.oz_s[k] = o[2 * k : 2 * k + 2]
        s.gz_s[...] = jnp.sum(s.gy_r[...], 0)
        s.gz_r[0] = s.gz_s[...]
        s.oz_r[0] = s.oz_s[z]

        @pl.loop(1, NZ)
        def _(k):
            zz = lax.rem(z + k, NZ)
            to = (y * NZ + zz, g)
            send(s.wz_s.at[zz], s.wz_r.at[k], s.wzs.at[0], s.wzr.at[0], to)
            send(s.oz_s.at[zz], s.oz_r.at[k], s.wzs.at[1], s.wzr.at[1], to)
            send(s.gz_s, s.gz_r.at[k], s.wzs.at[2], s.wzr.at[2], to)

    table_send(0)
    weights_y()
    table_send(1)
    weights_z()

    def table_finish(h):
        wait_all(s.tx_r.at[h, rest_x], s.txr.at[h])
        tgrad_ref[:, 256 * h : 256 * (h + 1)] = (
            s.tx_own[h] + s.tx_r[h, 1].astype(F32) + s.tx_r[h, 2].astype(F32) + s.tx_r[h, 3].astype(F32))

    table_finish(0)
    wait_all(s.oz_r.at[rest_z], s.wzr.at[1])
    s.og_s[...] = jnp.sum(s.oz_r[...], 0)
    s.og_r[0] = s.og_s[...]

    @pl.loop(1, 2 * NX)
    def _(k):
        send(s.og_s, s.og_r.at[k], s.ogs, s.ogr, (t, lax.rem(g + k, 2 * NX)))

    wait_all(s.wz_r.at[rest_z], s.wzr.at[0])
    wing_ref[...] = s.wz_own[z] + jnp.sum(s.wz_r[1:].astype(F32), 0)
    wait_all(s.gz_r.at[rest_z], s.wzr.at[2])
    total = jnp.sum(s.gz_r[...], 0)
    pick = jnp.where(iota((D, 128), 0) == 16 * t + iota((D, 128), 1), 1.0, 0.0)
    gaing_ref[...] = lax.dot_general(
        jnp.broadcast_to(total, (8, D)), pick, NN,
        precision=lax.Precision.HIGHEST, preferred_element_type=F32)[:1]
    wait_all(s.og_r.at[rest_g], s.ogr)
    woutg_ref[...] = jnp.concatenate([s.og_r[lax.rem(g + 2 * NX - k, 2 * NX)] for k in range(2 * NX)], 0)
    table_finish(1)

    wait_all(s.req.at[rest], s.rsend)
    wait_all(s.sbuf.at[rest], s.dsend)
    for h in range(CHUNKS):
        wait_all(s.obuf.at[h, rest], s.ssem.at[h])
        wait_all(s.tx_s.at[h, rest_x], s.txs.at[h])
        for dx in range(NX):
            wait_all(s.tc_s.at[h, dx], s.tcs.at[h, dx])
    for dx in range(NX):
        wait_all(s.wc_s.at[dx], s.wcs.at[dx])
    wait_all(s.oc_r, s.ocs)
    wait_all(s.gx_r.at[rest_g], s.gxs)
    wait_all(s.wx_s.at[rest_x], s.wxs.at[0])
    wait_all(s.ox_s.at[rest_x], s.wxs.at[1])
    wait_all(s.wy_s.at[rest_y], s.wys.at[0])
    wait_all(s.oy_s.at[rest_y], s.wys.at[1])
    wait_all(s.gy_r.at[rest_y], s.wys.at[2])
    wait_all(s.wz_s.at[rest_z], s.wzs.at[0])
    wait_all(s.oz_s.at[rest_z], s.wzs.at[1])
    wait_all(s.gz_r.at[rest_z], s.wzs.at[2])
    wait_all(s.og_r.at[rest_g], s.ogs)


def finish_kernel(res, tgrad, wing, woutg, gaing, res_o, tgrad_o, wing_o, woutg_o, gaing_o):
    res_o[...] = res[...]
    tgrad_o[...] = tgrad[...]
    wing_o[...] = wing[...]
    woutg_o[...] = woutg[...]
    gaing_o[...] = gaing[:, :16]


def on_device(item_owner, item_row, lengths, table, w_in, w_out, gain, cotangent):
    vm = pl.BlockSpec(memory_space=pltpu.VMEM)
    hbm = pl.BlockSpec(memory_space=pltpu.HBM)
    shapes = (
        jax.ShapeDtypeStruct((TOK, D), BF16),
        jax.ShapeDtypeStruct((256, D), F32),
        jax.ShapeDtypeStruct((16, 256), F32),
        jax.ShapeDtypeStruct((16, D), F32),
    )
    outs = pl.pallas_call(
        kernel,
        name="whole",
        out_shape=shapes + (jax.ShapeDtypeStruct((1, 128), F32),),
        in_specs=[pl.BlockSpec(memory_space=pltpu.SMEM)] + [hbm] * 7,
        out_specs=[vm] * 5,
        scratch_shapes=list(scratch().values()),
        compiler_params=pltpu.CompilerParams(
            collective_id=1, has_side_effects=True, vmem_limit_bytes=60 * 2**20
        ),
    )(lengths, item_owner.reshape(1, TOK), item_row.reshape(1, TOK), table, w_in, w_out,
      gain.reshape(1, D), cotangent)
    res, tgrad, wing, woutg, gaing = pl.pallas_call(
        finish_kernel,
        name="finish",
        out_shape=shapes + (jax.ShapeDtypeStruct((1, 16), F32),),
        in_specs=[vm] * 5,
        out_specs=[vm] * 5,
    )(*outs)
    return res, tgrad, wing, woutg, gaing.reshape(16)


def solution(mesh):
    return jax.shard_map(
        on_device,
        mesh=mesh,
        in_specs=(
            P(("table", "group"), None),
            P(("table", "group")),
            P(("table", "group"), None),
            P("table", None),
            P(),
            P(),
            P(),
            P(("table", "group"), None),
        ),
        out_specs=(
            P(("table", "group"), None),
            P(("table", "group"), None),
            P("table", "group"),
            P("table", None),
            P("table"),
        ),
        check_vma=False,
    )
```

```python
import types

import jax
import jax.numpy as jnp
from jax import lax
from jax.experimental import pallas as pl
from jax.experimental.pallas import tpu as pltpu
from jax.sharding import PartitionSpec as P

D = 512
TOK = 512
NY, NZ, NX = 4, 8, 4
NT_DEV = NY * NZ
CAP = 24
SLOTS = CAP * NT_DEV
CHUNKS = 4
WIDTH = D // CHUNKS
F32 = jnp.float32
BF16 = jnp.bfloat16
I32 = jnp.int32
NT = (((1,), (1,)), ((), ()))
TN = (((0,), (0,)), ((), ()))
NN = (((1,), (0,)), ((), ()))
MESH = pl.DeviceIdType.MESH
FAR_X = (2, 1, 3)


def dot(a, b, dims=NN):
    return lax.dot_general(a, b, dims, preferred_element_type=F32)


def iota(shape, axis):
    return lax.broadcasted_iota(I32, shape, axis)


def hot(cond):
    return jnp.where(cond, 1.0, 0.0).astype(BF16)


def half_lanes(v, half):
    lane = iota(v.shape, 1)
    keep = (lane < 64) if half == 0 else (lane >= 64)
    return jnp.where(keep, v, jnp.zeros_like(v))


def at_offset(t, k, sign):
    y, z = lax.div(t, NZ), lax.rem(t, NZ)
    dy, dz = lax.div(k, NZ), lax.rem(k, NZ)
    yy = lax.rem(y + sign * dy + NY, NY)
    zz = lax.rem(z + sign * dz + NZ, NZ)
    return yy * NZ + zz


def wait_all(ref, sem):
    pltpu.make_async_copy(ref, ref, sem).wait()


def send(src, dst, send_sem, recv_sem, to):
    pltpu.make_async_remote_copy(
        src_ref=src, dst_ref=dst, send_sem=send_sem, recv_sem=recv_sem,
        device_id=to, device_id_type=MESH,
    ).start()


def block(i, size):
    return pl.ds(pl.multiple_of(i * size, size), size)


def scratch():
    vm = pltpu.VMEM
    dma = pltpu.SemaphoreType.DMA
    return dict(
        own=vm((1, TOK), I32), row=vm((1, TOK), I32), table=vm((2048, D), BF16),
        w_in=vm((D, 2048), BF16), w_out=vm((D, D), BF16), cot=vm((TOK, D), BF16),
        gain=vm((1, D), F32),
        req=vm((NT_DEV, 1, 128), I32), got=vm((NT_DEV, 1, 128), I32),
        onehot=vm((24 * NZ, 2048), BF16), sbuf=vm((NT_DEV, CAP, D), BF16),
        rbuf=vm((NT_DEV, CAP, D), BF16), place=vm((SLOTS, TOK), BF16),
        hot=vm((2048, SLOTS), BF16),
        emb=vm((TOK, D), BF16), emb_t=vm((D, TOK), BF16), w_in_t=vm((2048, D), BF16),
        slope=vm((TOK, 2048), F32), proj=vm((TOK, 2048), BF16), w=vm((8, TOK, TOK), BF16),
        d=vm((8, TOK, TOK), F32), mask=vm((TOK, TOK), F32), att=vm((TOK, D), F32),
        gmix=vm((TOK, D), F32), gatt=vm((TOK, D), BF16), gpre=vm((TOK, 2048), BF16),
        mixed=vm((TOK, D), BF16), gacc=vm((2, 256, 128), F32), gemb=vm((TOK, D), BF16),
        order=vm((D, D), BF16), gwout=vm((D, D), BF16), ggain=vm((1, D), F32),
        obuf=vm((CHUNKS, NT_DEV, CAP, WIDTH), BF16), ibuf=vm((CHUNKS, NT_DEV, CAP, WIDTH), BF16),
        tc_s=vm((CHUNKS, NX, 256, WIDTH), BF16), tc_r=vm((CHUNKS, NX, 256, WIDTH), BF16),
        tx_s=vm((CHUNKS, NX, 256, WIDTH), BF16), tx_r=vm((CHUNKS, NX, 256, WIDTH), BF16),
        tx_own=vm((CHUNKS, 256, WIDTH), F32),
        wc_s=vm((NX, D, 256), BF16), wc_r=vm((NX, D, 256), BF16), oc_r=vm((NX, 64, D), BF16),
        wx_s=vm((NX, D, 256), BF16), wx_r=vm((NX, D, 256), BF16), wf=vm((NX, D, 256), F32), wh_s=vm((2, 256, 256), BF16), wh_r=vm((2, 256, 256), BF16),
        ox_s=vm((NX, 64, D), BF16), ox_r=vm((NX, 64, D), BF16), ox_own=vm((64, D), F32),
        gx_r=vm((2 * NX, 1, D), F32),
        wy_s=vm((NY, 128, 256), BF16), wy_r=vm((NY, 128, 256), BF16), wy_own=vm((NY, 128, 256), F32),
        oy_s=vm((NY, 16, D), BF16), oy_r=vm((NY, 16, D), BF16), oy_own=vm((NY, 16, D), F32),
        gy_s=vm((1, D), F32), gy_r=vm((NY, 1, D), F32),
        wz_s=vm((NZ, 16, 256), BF16), wz_r=vm((NZ, 16, 256), BF16), wz_own=vm((NZ, 16, 256), F32),
        oz_s=vm((NZ, 2, D), F32), oz_r=vm((NZ, 2, D), F32),
        gz_s=vm((1, D), F32), gz_r=vm((NZ, 1, D), F32),
        og_s=vm((2, D), F32), og_r=vm((2 * NX, 2, D), F32),
        load=dma((7,)), rsend=dma, rrecv=dma((NY,)), dsend=dma, drecv=dma,
        ssem=dma((CHUNKS,)), isem=dma((CHUNKS,)),
        tcs=dma((CHUNKS, NX)), tcr=dma((CHUNKS, NX)), txs=dma((CHUNKS,)), txr=dma((CHUNKS,)),
        wcs=dma((NX,)), wcr=dma((NX,)), ocs=dma, ocr=dma, gxs=dma, gxr=dma,
        wxs=dma((NX,)), wxr=dma((NX,)), whs=dma((2,)), whr=dma((2,)), oxs=dma, oxr=dma, wys=dma((3,)), wyr=dma((3,)), wzs=dma((3,)), wzr=dma((3,)),
        ogs=dma, ogr=dma,
    )


def kernel(len_ref, own_h, row_h, table_h, w_in_h, w_out_h, gain_h, cot_h,
           res_ref, tgrad_ref, wing_ref, woutg_ref, gaing_ref, *refs):
    s = types.SimpleNamespace(**dict(zip(scratch(), refs)))
    t, g = lax.axis_index("table"), lax.axis_index("group")
    x, c = lax.div(g, 2), lax.rem(g, 2)
    other = 1 - c
    y, z = lax.div(t, NZ), lax.rem(t, NZ)
    partner = (t, x * 2 + other)
    barrier = pltpu.get_barrier_semaphore()

    loads = [
        pltpu.make_async_copy(src, dst, s.load.at[i])
        for i, (src, dst) in enumerate((
            (own_h, s.own), (row_h, s.row), (table_h, s.table), (w_out_h, s.w_out),
            (cot_h, s.cot), (w_in_h, s.w_in), (gain_h, s.gain)))
    ]
    for copy in loads:
        copy.start()

    @pl.loop(1, NT_DEV)
    def _(k):
        pl.semaphore_signal(
            barrier, inc=1, device_id=(at_offset(t, NT_DEV - k, 1), g), device_id_type=MESH)

    @pl.loop(1, 2 * NX)
    def _(k):
        pl.semaphore_signal(
            barrier, inc=1, device_id=(t, lax.rem(g + k, 2 * NX)), device_id_type=MESH)

    def x_of(dx):
        return lax.rem(x + dx, NX)

    loads[0].wait()
    loads[1].wait()
    own = s.own[...]
    rel = ((lax.shift_right_logical(own, 3) - y) & (NY - 1)) * NZ + (((own & (NZ - 1)) - z) & (NZ - 1))
    is_rel = rel == iota((NT_DEV, TOK), 0)
    before = dot(hot(is_rel), hot(iota((TOK, TOK), 0) < iota((TOK, TOK), 1)))
    rank = jnp.sum(jnp.where(is_rel, before, 0.0), 0, keepdims=True).astype(I32)
    idx = s.row[...] + 1
    ranks = hot(rank == iota((128, TOK), 0))
    high = jnp.where(is_rel, lax.shift_right_logical(idx, 6).astype(F32), 0.0).astype(BF16)
    low = jnp.where(is_rel, (idx & 63).astype(F32), 0.0).astype(BF16)
    wanted = dot(high, ranks, NT) * 64.0 + dot(low, ranks, NT)
    s.req[...] = wanted.astype(I32).reshape(NT_DEV, 1, 128)
    s.got[0] = s.req[0]

    pl.semaphore_wait(barrier, NT_DEV - 1 + 2 * NX - 1)

    @pl.loop(1, NT_DEV)
    def _(i):
        k = NT_DEV - i
        send(s.req.at[k], s.got.at[k], s.rsend, s.rrecv.at[lax.div(k, NZ)], (at_offset(t, k, 1), g))

    s.place[...] = hot(rel * CAP + rank == iota((SLOTS, TOK), 0))
    loads[2].wait()

    for b in (3, 2, 1, 0):
        first = 1 if b == 0 else 0
        wait_all(s.got.at[pl.ds(NZ * b + first, NZ - first)], s.rrecv.at[b])
        names = jnp.transpose(s.got[NZ * b : NZ * (b + 1), 0, :].astype(F32))
        col = jnp.concatenate(
            [names[:CAP, j : j + 1] for j in range(NZ)], 0).astype(I32)
        for q in range(4):
            s.onehot[:, 512 * q : 512 * (q + 1)] = hot(col == 512 * q + 1 + iota((24 * NZ, 512), 1))
        rows = dot(s.onehot[...], s.table[...])
        message = rows.reshape(NZ, CAP, D).astype(BF16)
        s.sbuf[NZ * b : NZ * (b + 1)] = message
        if b == 0:
            s.rbuf[0] = message[0]

        @pl.loop(first, NZ)
        def _(i):
            k = NZ * b + (NZ - 1 + first - i)
            send(s.sbuf.at[k], s.rbuf.at[k], s.dsend, s.drecv, (at_offset(t, k, -1), g))

    ids = s.got[:, 0, :]
    high = lax.shift_right_logical(ids, 6).astype(F32).astype(BF16)
    low = (ids & 63).astype(F32).astype(BF16)

    lane = iota((NT_DEV, SLOTS), 1)
    source = jnp.floor((lane.astype(F32) + 0.5) * (1.0 / CAP)).astype(I32)
    lane = iota((128, SLOTS), 1)
    turn = lane - CAP * jnp.floor((lane.astype(F32) + 0.5) * (1.0 / CAP)).astype(I32)
    pick = hot(iota((128, SLOTS), 0) == turn)
    both = dot(high, pick) * 64.0 + dot(low, pick)
    mine = iota((NT_DEV, SLOTS), 0) == source
    name = jnp.sum(jnp.where(mine, both, 0.0), 0, keepdims=True).astype(I32)

    @pl.loop(0, 8)
    def _(i):
        s.hot[block(i, 256), :] = hot(name == i * 256 + 1 + iota((256, SLOTS), 0))

    ends = []
    total = jnp.int32(0)
    for k in range(8):
        total = total + len_ref[0, k]
        ends.append(total)
    for r in range(4):
        pos = 128 * r + iota((128, 128), 0)
        start = jnp.zeros((128, 128), I32)
        for e in ends:
            start = jnp.where(pos >= e, e, start)
        for q in range(4):
            col = 128 * q + iota((128, 128), 1)
            ok = (col >= start) & (col <= pos)
            s.mask[128 * r : 128 * (r + 1), 128 * q : 128 * (q + 1)] = jnp.where(ok, 1.0, 0.0)

    loads[3].wait()
    loads[4].wait()

    @pl.loop(0, 4)
    def _(r):
        rows = block(r, 128)
        s.gmix[rows, :] = dot(s.cot[rows, :], s.w_out[...], NT).astype(BF16).astype(F32)

    lane = iota((D, D), 1)
    source = ((lane >> 1) & 31) * 16 + (lane >> 6) * 2 + (lane & 1)
    s.order[...] = hot(iota((D, D), 0) == source)
    loads[5].wait()
    loads[6].wait()

    @pl.loop(0, 8)
    def _(q):
        s.w_in_t[block(q, 256), :] = jnp.transpose(s.w_in[:, block(q, 256)])

    rest = pl.ds(1, NT_DEV - 1)
    wait_all(s.rbuf.at[rest], s.drecv)
    s.emb[...] = dot(s.place[...], s.rbuf[...].reshape(SLOTS, D), TN).astype(BF16)

    @pl.loop(0, 8)
    def _(q):
        cols = block(q, 256)
        for r in range(2):
            rows = pl.ds(256 * r, 256)
            pre = dot(s.emb[rows, :], s.w_in[:, cols])
            sig = 0.5 + 0.5 * jnp.tanh(0.5 * pre)
            act = pre * sig
            s.proj[rows, cols] = act.astype(BF16)
            s.slope[rows, cols] = sig + act * (1.0 - sig)

    @pl.loop(0, 4)
    def _(p):
        off = pl.multiple_of(p * 128, 128)
        for r in range(2):
            rows = pl.ds(256 * r, 256)
            cols = pl.ds(0, 256 * (r + 1))
            key = s.proj[cols, pl.ds(1536 + off, 128)]
            val = s.proj[cols, pl.ds(512 + off, 128)]
            qry = s.proj[rows, pl.ds(1024 + off, 128)] * jnp.asarray(0.0625, BF16)
            mask = s.mask[rows, cols]
            acc = None
            for half in range(2):
                h = dot(half_lanes(qry, half), key, NT)
                th = jnp.tanh(h)
                um = (1.0 + th) * mask
                w = h * um
                s.d[2 * p + half, rows, cols] = um + w * (1.0 - th)
                wb = w.astype(BF16)
                s.w[2 * p + half, rows, cols] = wb
                part = dot(wb, half_lanes(val, half))
                acc = part if acc is None else acc + part
            s.att[rows, pl.ds(off, 128)] = acc

    s.ggain[...] = jnp.zeros_like(s.ggain)

    @pl.loop(0, 4)
    def _(r):
        rows = block(r, 128)
        att = s.att[rows, :]
        cen = att - jnp.mean(att, 1, keepdims=True)
        inv = lax.rsqrt(jnp.mean(cen * cen, 1, keepdims=True) + 1e-05)
        normed = cen * inv
        gain = s.gain[...]
        upd = s.proj[rows, pl.ds(0, 512)].astype(F32)
        s.mixed[rows, :] = (normed * gain * upd).astype(BF16)
        gmix = s.gmix[rows, :]
        gn = gmix * normed
        s.gpre[rows, pl.ds(0, 512)] = (gn * gain * s.slope[rows, pl.ds(0, 512)]).astype(BF16)
        s.ggain[...] += jnp.sum(gn * upd, 0, keepdims=True)
        gnorm = gmix * gain * upd
        m1 = jnp.mean(gnorm, 1, keepdims=True)
        m2 = jnp.mean(gnorm * normed, 1, keepdims=True)
        s.gatt[rows, :] = ((gnorm - m1 - normed * m2) * inv).astype(BF16)

    mixed = dot(s.mixed[...], s.order[...]).astype(BF16)
    s.gwout[...] = dot(mixed, s.cot[...], TN).astype(BF16)
    s.gx_r[0] = s.ggain[...]

    @pl.loop(0, NX)
    def _(dx):
        send(s.gwout.at[block(x_of(dx) * 2 + other, 64), :], s.oc_r.at[dx], s.ocs, s.ocr, partner)

    @pl.loop(1, 2 * NX)
    def _(k):
        send(s.ggain, s.gx_r.at[k], s.gxs, s.gxr, (t, lax.rem(g + k, 2 * NX)))

    def back_pair(p):
        off = pl.multiple_of(p * 128, 128)
        for r in range(2):
            rows = pl.ds(256 * r, 256)
            cols = pl.ds(0, 256 * (r + 1))
            key = s.proj[cols, pl.ds(1536 + off, 128)] * jnp.asarray(0.0625, BF16)
            val = s.proj[cols, pl.ds(512 + off, 128)]
            qry = s.proj[rows, pl.ds(1024 + off, 128)] * jnp.asarray(0.0625, BF16)
            gat = s.gatt[rows, pl.ds(off, 128)]
            gq = gk = gv = None
            for half in range(2):
                gath = half_lanes(gat, half)
                gw = dot(gath, val, NT)
                gs = (gw * s.d[2 * p + half, rows, cols]).astype(BF16)
                a = dot(gs, half_lanes(key, half))
                b = dot(gs, half_lanes(qry, half), TN)
                v = dot(s.w[2 * p + half, rows, cols], gath, TN)
                gq = a if gq is None else gq + a
                gk = b if gk is None else gk + b
                gv = v if gv is None else gv + v
            qcols = pl.ds(1024 + off, 128)
            s.gpre[rows, qcols] = (gq * s.slope[rows, qcols]).astype(BF16)
            if r == 0:
                s.gacc[0] = gk
                s.gacc[1] = gv
            else:
                for n, acc in ((0, gk), (1, gv)):
                    dst = pl.ds((1536 if n == 0 else 512) + off, 128)
                    for half in range(2):
                        part = pl.ds(256 * half, 256)
                        v = acc[256 * half : 256 * (half + 1)]
                        v = v + s.gacc[n] if half == 0 else v
                        s.gpre[part, dst] = (v * s.slope[part, dst]).astype(BF16)

    pl.loop(0, 2)(back_pair)
    wait_all(s.oc_r, s.ocr)
    for dx in FAR_X + (0,):
        o = s.gwout[block(x_of(dx) * 2 + c, 64), :].astype(F32) + s.oc_r[dx].astype(F32)
        if dx:
            s.ox_s[dx] = o.astype(BF16)
            send(s.ox_s.at[dx], s.ox_r.at[dx], s.oxs, s.oxr, (t, x_of(dx) * 2 + c))
        else:
            s.ox_own[...] = o
    pl.loop(2, 4)(back_pair)

    @pl.loop(0, 2)
    def _(r):
        rows = block(r, 256)
        v = dot(s.gpre[rows, :], s.w_in_t[...])
        s.gemb[rows, :] = (s.cot[rows, :].astype(F32) + v).astype(BF16)

    for n in range(2):
        out = dot(s.place[...], s.gemb[:, 256 * n : 256 * (n + 1)])
        for h in range(2 * n, 2 * n + 2):
            part = out[:, WIDTH * (h - 2 * n) : WIDTH * (h - 2 * n + 1)]
            message = part.reshape(NT_DEV, CAP, WIDTH).astype(BF16)
            s.obuf[h] = message
            s.ibuf[h, 0] = message[0]

            @pl.loop(1, NT_DEV)
            def _(i):
                k = NT_DEV - i
                send(s.obuf.at[h, k], s.ibuf.at[h, k], s.ssem.at[h], s.isem.at[h],
                     (at_offset(t, k, 1), g))

    rest_x, rest_y, rest_z = pl.ds(1, NX - 1), pl.ds(1, NY - 1), pl.ds(1, NZ - 1)
    rest_g = pl.ds(1, 2 * NX - 1)

    def outer_y():
        wait_all(s.ox_r.at[rest_x], s.oxr)
        wait_all(s.gx_r.at[rest_g], s.gxr)
        o = s.ox_own[...] + s.ox_r[1].astype(F32) + s.ox_r[2].astype(F32) + s.ox_r[3].astype(F32)
        s.oy_own[...] = o.reshape(NY, 16, D)
        s.oy_s[...] = o.astype(BF16).reshape(NY, 16, D)
        s.gy_s[...] = jnp.sum(s.gx_r[...], 0)
        s.gy_r[0] = s.gy_s[...]

        @pl.loop(1, NY)
        def _(k):
            yy = lax.rem(y + k, NY)
            to = (yy * NZ + z, g)
            send(s.oy_s.at[yy], s.oy_r.at[k], s.wys.at[1], s.wyr.at[1], to)
            send(s.gy_s, s.gy_r.at[k], s.wys.at[2], s.wyr.at[2], to)

    def outer_z():
        wait_all(s.oy_r.at[rest_y], s.wyr.at[1])
        wait_all(s.gy_r.at[rest_y], s.wyr.at[2])
        o = s.oy_own[y] + s.oy_r[1].astype(F32) + s.oy_r[2].astype(F32) + s.oy_r[3].astype(F32)
        for k in range(NZ):
            s.oz_s[k] = o[2 * k : 2 * k + 2]
        s.gz_s[...] = jnp.sum(s.gy_r[...], 0)
        s.gz_r[0] = s.gz_s[...]
        s.oz_r[0] = s.oz_s[z]

        @pl.loop(1, NZ)
        def _(k):
            zz = lax.rem(z + k, NZ)
            to = (y * NZ + zz, g)
            send(s.oz_s.at[zz], s.oz_r.at[k], s.wzs.at[1], s.wzr.at[1], to)
            send(s.gz_s, s.gz_r.at[k], s.wzs.at[2], s.wzr.at[2], to)

    def outer_g():
        wait_all(s.oz_r.at[rest_z], s.wzr.at[1])
        s.og_s[...] = jnp.sum(s.oz_r[...], 0)
        s.og_r[0] = s.og_s[...]

        @pl.loop(1, 2 * NX)
        def _(k):
            send(s.og_s, s.og_r.at[k], s.ogs, s.ogr, (t, lax.rem(g + k, 2 * NX)))

        wait_all(s.gz_r.at[rest_z], s.wzr.at[2])
        total = jnp.sum(s.gz_r[...], 0)
        pick = jnp.where(iota((D, 128), 0) == 16 * t + iota((D, 128), 1), 1.0, 0.0)
        gaing_ref[...] = lax.dot_general(
            jnp.broadcast_to(total, (8, D)), pick, NN,
            precision=lax.Precision.HIGHEST, preferred_element_type=F32)[:1]

    def inner_core():
        s.emb_t[...] = jnp.transpose(s.emb[...])
        for dx in FAR_X + (0,):
            cols = block(x_of(dx) * 2 + other, 256)
            s.wc_s[dx] = dot(s.emb_t[...], s.gpre[:, cols]).astype(BF16)
            send(s.wc_s.at[dx], s.wc_r.at[dx], s.wcs.at[dx], s.wcr.at[dx], partner)
        for dx in FAR_X + (0,):
            w = dot(s.emb_t[...], s.gpre[:, block(x_of(dx) * 2 + c, 256)])
            wait_all(s.wc_r.at[dx], s.wcr.at[dx])
            w = w + s.wc_r[dx].astype(F32)
            if dx == 2:
                for n, to in ((0, 1), (1, 3)):
                    s.wh_s[n] = w[256 * n : 256 * (n + 1)].astype(BF16)
                    send(s.wh_s.at[n], s.wh_r.at[n], s.whs.at[n], s.whr.at[n],
                         (t, x_of(to) * 2 + c))
            else:
                s.wf[dx] = w

    def inner_x():
        for n, dx in ((0, 1), (1, 3)):
            wait_all(s.wh_r.at[n], s.whr.at[n])
            near, far = pl.ds(256 * n, 256), pl.ds(256 * (1 - n), 256)
            s.wx_s[dx, near, :] = (s.wf[dx, near, :] + s.wh_r[n].astype(F32)).astype(BF16)
            s.wx_s[dx, far, :] = s.wf[dx, far, :].astype(BF16)
            send(s.wx_s.at[dx], s.wx_r.at[dx], s.wxs.at[dx], s.wxr.at[dx], (t, x_of(dx) * 2 + c))

    def inner_y():
        wait_all(s.wx_r.at[1], s.wxr.at[1])
        wait_all(s.wx_r.at[3], s.wxr.at[3])
        w = s.wf[0] + s.wx_r[1].astype(F32) + s.wx_r[3].astype(F32)
        s.wy_own[...] = w.reshape(NY, 128, 256)
        s.wy_s[...] = w.astype(BF16).reshape(NY, 128, 256)

        @pl.loop(1, NY)
        def _(k):
            yy = lax.rem(y + k, NY)
            send(s.wy_s.at[yy], s.wy_r.at[k], s.wys.at[0], s.wyr.at[0], (yy * NZ + z, g))

    def inner_z():
        wait_all(s.wy_r.at[rest_y], s.wyr.at[0])
        w = s.wy_own[y] + s.wy_r[1].astype(F32) + s.wy_r[2].astype(F32) + s.wy_r[3].astype(F32)
        s.wz_own[...] = w.reshape(NZ, 16, 256)
        s.wz_s[...] = w.astype(BF16).reshape(NZ, 16, 256)

        @pl.loop(1, NZ)
        def _(k):
            zz = lax.rem(z + k, NZ)
            send(s.wz_s.at[zz], s.wz_r.at[k], s.wzs.at[0], s.wzr.at[0], (y * NZ + zz, g))

    def table_send(h):
        wait_all(s.ibuf.at[h, rest], s.isem.at[h])

        def table_rows(which):
            return dot(s.hot[block(which, 256), :], s.ibuf[h].reshape(SLOTS, WIDTH))

        for dx in FAR_X + (0,):
            s.tc_s[h, dx] = table_rows(x_of(dx) * 2 + other).astype(BF16)
            send(s.tc_s.at[h, dx], s.tc_r.at[h, dx], s.tcs.at[h, dx], s.tcr.at[h, dx], partner)
        for dx in FAR_X + (0,):
            own = table_rows(x_of(dx) * 2 + c)
            wait_all(s.tc_r.at[h, dx], s.tcr.at[h, dx])
            own = own + s.tc_r[h, dx].astype(F32)
            if dx:
                s.tx_s[h, dx] = own.astype(BF16)
                send(s.tx_s.at[h, dx], s.tx_r.at[h, dx], s.txs.at[h], s.txr.at[h],
                     (t, x_of(dx) * 2 + c))
            else:
                s.tx_own[h] = own

    def table_finish(h):
        wait_all(s.tx_r.at[h, rest_x], s.txr.at[h])
        tgrad_ref[:, WIDTH * h : WIDTH * (h + 1)] = (
            s.tx_own[h] + s.tx_r[h, 1].astype(F32) + s.tx_r[h, 2].astype(F32) + s.tx_r[h, 3].astype(F32))

    outer_y()
    inner_core()

    @pl.loop(0, 4)
    def _(r):
        rows = block(r, 128)
        out = dot(s.mixed[rows, :], s.w_out[...])
        res_ref[rows, :] = (s.emb[rows, :].astype(F32) + out).astype(BF16)

    inner_x()
    outer_z()
    table_send(0)
    outer_g()
    table_send(1)
    inner_y()
    table_send(2)
    inner_z()
    table_send(3)
    wait_all(s.og_r.at[rest_g], s.ogr)
    woutg_ref[...] = jnp.concatenate([s.og_r[lax.rem(g + 2 * NX - k, 2 * NX)] for k in range(2 * NX)], 0)
    wait_all(s.wz_r.at[rest_z], s.wzr.at[0])
    wing_ref[...] = s.wz_own[z] + jnp.sum(s.wz_r[1:].astype(F32), 0)
    for h in range(CHUNKS):
        table_finish(h)

    wait_all(s.req.at[rest], s.rsend)
    wait_all(s.sbuf.at[rest], s.dsend)
    for h in range(CHUNKS):
        wait_all(s.obuf.at[h, rest], s.ssem.at[h])
        wait_all(s.tx_s.at[h, rest_x], s.txs.at[h])
        for dx in range(NX):
            wait_all(s.tc_s.at[h, dx], s.tcs.at[h, dx])
    for dx in range(NX):
        wait_all(s.wc_s.at[dx], s.wcs.at[dx])
    wait_all(s.oc_r, s.ocs)
    wait_all(s.gx_r.at[rest_g], s.gxs)
    for n, dx in ((0, 1), (1, 3)):
        wait_all(s.wh_s.at[n], s.whs.at[n])
        wait_all(s.wx_s.at[dx], s.wxs.at[dx])
    wait_all(s.ox_s.at[rest_x], s.oxs)
    wait_all(s.wy_s.at[rest_y], s.wys.at[0])
    wait_all(s.oy_s.at[rest_y], s.wys.at[1])
    wait_all(s.gy_r.at[rest_y], s.wys.at[2])
    wait_all(s.wz_s.at[rest_z], s.wzs.at[0])
    wait_all(s.oz_s.at[rest_z], s.wzs.at[1])
    wait_all(s.gz_r.at[rest_z], s.wzs.at[2])
    wait_all(s.og_r.at[rest_g], s.ogs)


def finish_kernel(res, tgrad, wing, woutg, gaing, res_o, tgrad_o, wing_o, woutg_o, gaing_o):
    res_o[...] = res[...]
    tgrad_o[...] = tgrad[...]
    wing_o[...] = wing[...]
    woutg_o[...] = woutg[...]
    gaing_o[...] = gaing[:, :16]


def on_device(item_owner, item_row, lengths, table, w_in, w_out, gain, cotangent):
    vm = pl.BlockSpec(memory_space=pltpu.VMEM)
    hbm = pl.BlockSpec(memory_space=pltpu.HBM)
    shapes = (
        jax.ShapeDtypeStruct((TOK, D), BF16),
        jax.ShapeDtypeStruct((256, D), F32),
        jax.ShapeDtypeStruct((16, 256), F32),
        jax.ShapeDtypeStruct((16, D), F32),
    )
    outs = pl.pallas_call(
        kernel,
        name="whole",
        out_shape=shapes + (jax.ShapeDtypeStruct((1, 128), F32),),
        in_specs=[pl.BlockSpec(memory_space=pltpu.SMEM)] + [hbm] * 7,
        out_specs=[vm] * 5,
        scratch_shapes=list(scratch().values()),
        compiler_params=pltpu.CompilerParams(
            collective_id=1, has_side_effects=True, vmem_limit_bytes=60 * 2**20
        ),
    )(lengths, item_owner.reshape(1, TOK), item_row.reshape(1, TOK), table, w_in, w_out,
      gain.reshape(1, D), cotangent)
    res, tgrad, wing, woutg, gaing = pl.pallas_call(
        finish_kernel,
        name="finish",
        out_shape=shapes + (jax.ShapeDtypeStruct((1, 16), F32),),
        in_specs=[vm] * 5,
        out_specs=[vm] * 5,
    )(*outs)
    return res, tgrad, wing, woutg, gaing.reshape(16)


def solution(mesh):
    return jax.shard_map(
        on_device,
        mesh=mesh,
        in_specs=(
            P(("table", "group"), None),
            P(("table", "group")),
            P(("table", "group"), None),
            P("table", None),
            P(),
            P(),
            P(),
            P(("table", "group"), None),
        ),
        out_specs=(
            P(("table", "group"), None),
            P(("table", "group"), None),
            P("table", "group"),
            P("table", None),
            P("table"),
        ),
        check_vma=False,
    )
```

```python
import types

import jax
import jax.numpy as jnp
from jax import lax
from jax.experimental import pallas as pl
from jax.experimental.pallas import tpu as pltpu
from jax.sharding import PartitionSpec as P

D = 512
TOK = 512
NY, NZ, NX = 4, 8, 4
NT_DEV = NY * NZ
CAP = 24
SLOTS = CAP * NT_DEV
WIDTHS = (256, 128, 128)
STARTS = (0, 256, 384)
CHUNKS = len(WIDTHS)
F32 = jnp.float32
BF16 = jnp.bfloat16
I32 = jnp.int32
NT = (((1,), (1,)), ((), ()))
TN = (((0,), (0,)), ((), ()))
NN = (((1,), (0,)), ((), ()))
MESH = pl.DeviceIdType.MESH
FAR_X = (2, 1, 3)


def dot(a, b, dims=NN):
    return lax.dot_general(a, b, dims, preferred_element_type=F32)


def iota(shape, axis):
    return lax.broadcasted_iota(I32, shape, axis)


def hot(cond):
    return jnp.where(cond, 1.0, 0.0).astype(BF16)


def half_lanes(v, half):
    lane = iota(v.shape, 1)
    keep = (lane < 64) if half == 0 else (lane >= 64)
    return jnp.where(keep, v, jnp.zeros_like(v))


def at_offset(t, k, sign):
    y, z = lax.div(t, NZ), lax.rem(t, NZ)
    step, dy = lax.div(k, NY), lax.rem(k, NY)
    half = lax.div(step + 1, 2)
    dz = jnp.where(lax.rem(step, 2) == 1, half, NZ - half)
    yy = lax.rem(y + sign * dy + NY, NY)
    zz = lax.rem(z + sign * dz + NZ, NZ)
    return yy * NZ + zz


def wait_all(ref, sem):
    pltpu.make_async_copy(ref, ref, sem).wait()


def send(src, dst, send_sem, recv_sem, to):
    pltpu.make_async_remote_copy(
        src_ref=src, dst_ref=dst, send_sem=send_sem, recv_sem=recv_sem,
        device_id=to, device_id_type=MESH,
    ).start()


def block(i, size):
    return pl.ds(pl.multiple_of(i * size, size), size)


def scratch():
    vm = pltpu.VMEM
    dma = pltpu.SemaphoreType.DMA
    return dict(
        own=vm((1, TOK), I32), row=vm((1, TOK), I32), table=vm((2048, D), BF16),
        w_in=vm((D, 2048), BF16), w_out=vm((D, D), BF16), cot=vm((TOK, D), BF16),
        gain=vm((1, D), F32),
        req=vm((NT_DEV, 1, 128), I32), got=vm((NT_DEV, 1, 128), I32),
        onehot=vm((24 * NZ, 2048), BF16), sbuf=vm((NT_DEV, CAP, D), BF16),
        rbuf=vm((NT_DEV, CAP, D), BF16), place=vm((SLOTS, TOK), BF16),
        hot=vm((2048, SLOTS), BF16),
        emb=vm((TOK, D), BF16), emb_t=vm((D, TOK), BF16), w_in_t=vm((2048, D), BF16),
        slope=vm((TOK, 2048), F32), proj=vm((TOK, 2048), BF16), w=vm((8, TOK, TOK), BF16),
        d=vm((8, TOK, TOK), F32), mask=vm((TOK, TOK), F32), att=vm((TOK, D), F32),
        gmix=vm((TOK, D), F32), gatt=vm((TOK, D), BF16), gpre=vm((TOK, 2048), BF16),
        mixed=vm((TOK, D), BF16), gacc=vm((2, 256, 128), F32), gemb=vm((TOK, D), BF16),
        order=vm((D, D), BF16), gwout=vm((D, D), BF16), ggain=vm((1, D), F32),
        **{f"obuf{h}": vm((NT_DEV, CAP, w), BF16) for h, w in enumerate(WIDTHS)},
        **{f"ibuf{h}": vm((NT_DEV, CAP, w), BF16) for h, w in enumerate(WIDTHS)},
        **{f"{n}{h}": vm((NX, 256, w), BF16) for h, w in enumerate(WIDTHS)
           for n in ("tc_s", "tc_r", "tx_s", "tx_r")},
        **{f"tx_own{h}": vm((256, w), F32) for h, w in enumerate(WIDTHS)},
        wc_s=vm((NX, D, 256), BF16), wc_r=vm((NX, D, 256), BF16), oc_r=vm((NX, 64, D), BF16),
        wx_s=vm((NX, D, 256), BF16), wx_r=vm((NX, D, 256), BF16), wf=vm((NX, D, 256), F32), wh_s=vm((2, 256, 256), BF16), wh_r=vm((2, 256, 256), BF16),
        ox_s=vm((NX, 64, D), BF16), ox_r=vm((NX, 64, D), BF16), ox_own=vm((64, D), F32),
        gx_r=vm((2 * NX, 1, D), F32),
        wy_s=vm((NY, 128, 256), BF16), wy_r=vm((NY, 128, 256), BF16), wy_own=vm((NY, 128, 256), F32),
        oy_s=vm((NY, 16, D), BF16), oy_r=vm((NY, 16, D), BF16), oy_own=vm((NY, 16, D), F32),
        gy_s=vm((1, D), F32), gy_r=vm((NY, 1, D), F32),
        wz_s=vm((NZ, 16, 256), BF16), wz_r=vm((NZ, 16, 256), BF16), wz_own=vm((NZ, 16, 256), F32),
        oz_s=vm((NZ, 2, D), F32), oz_r=vm((NZ, 2, D), F32),
        gz_s=vm((1, D), F32), gz_r=vm((NZ, 1, D), F32),
        og_s=vm((2, D), F32), og_r=vm((2 * NX, 2, D), F32),
        load=dma((7,)), rsend=dma, rrecv=dma((NY,)), dsend=dma, drecv=dma,
        ssem=dma((CHUNKS,)), isem=dma((CHUNKS,)),
        tcs=dma((CHUNKS, NX)), tcr=dma((CHUNKS, NX)), txs=dma((CHUNKS,)), txr=dma((CHUNKS,)),
        wcs=dma((NX,)), wcr=dma((NX,)), ocs=dma, ocr=dma, gxs=dma, gxr=dma,
        wxs=dma((NX,)), wxr=dma((NX,)), whs=dma((2,)), whr=dma((2,)), oxs=dma, oxr=dma, wys=dma((3,)), wyr=dma((3,)), wzs=dma((3,)), wzr=dma((3,)),
        ogs=dma, ogr=dma,
    )


def kernel(len_ref, own_h, row_h, table_h, w_in_h, w_out_h, gain_h, cot_h,
           res_ref, tgrad_ref, wing_ref, woutg_ref, gaing_ref, *refs):
    s = types.SimpleNamespace(**dict(zip(scratch(), refs)))

    def part(name, h):
        return getattr(s, name + str(h))

    t, g = lax.axis_index("table"), lax.axis_index("group")
    x, c = lax.div(g, 2), lax.rem(g, 2)
    other = 1 - c
    y, z = lax.div(t, NZ), lax.rem(t, NZ)
    partner = (t, x * 2 + other)
    barrier = pltpu.get_barrier_semaphore()

    loads = [
        pltpu.make_async_copy(src, dst, s.load.at[i])
        for i, (src, dst) in enumerate((
            (own_h, s.own), (row_h, s.row), (table_h, s.table), (w_out_h, s.w_out),
            (cot_h, s.cot), (w_in_h, s.w_in), (gain_h, s.gain)))
    ]
    for copy in loads:
        copy.start()

    @pl.loop(1, NT_DEV)
    def _(k):
        pl.semaphore_signal(
            barrier, inc=1, device_id=(at_offset(t, NT_DEV - k, 1), g), device_id_type=MESH)

    @pl.loop(1, 2 * NX)
    def _(k):
        pl.semaphore_signal(
            barrier, inc=1, device_id=(t, lax.rem(g + k, 2 * NX)), device_id_type=MESH)

    def x_of(dx):
        return lax.rem(x + dx, NX)

    loads[0].wait()
    loads[1].wait()
    own = s.own[...]
    dy = (lax.shift_right_logical(own, 3) - y) & (NY - 1)
    dz = ((own & (NZ - 1)) - z) & (NZ - 1)
    step = jnp.where(dz == 0, 0, jnp.where(dz <= NZ // 2, 2 * dz - 1, 2 * (NZ - dz)))
    rel = step * NY + dy
    is_rel = rel == iota((NT_DEV, TOK), 0)
    before = dot(hot(is_rel), hot(iota((TOK, TOK), 0) < iota((TOK, TOK), 1)))
    rank = jnp.sum(jnp.where(is_rel, before, 0.0), 0, keepdims=True).astype(I32)
    idx = s.row[...] + 1
    ranks = hot(rank == iota((128, TOK), 0))
    high = jnp.where(is_rel, lax.shift_right_logical(idx, 6).astype(F32), 0.0).astype(BF16)
    low = jnp.where(is_rel, (idx & 63).astype(F32), 0.0).astype(BF16)
    wanted = dot(high, ranks, NT) * 64.0 + dot(low, ranks, NT)
    s.req[...] = wanted.astype(I32).reshape(NT_DEV, 1, 128)
    s.got[0] = s.req[0]

    pl.semaphore_wait(barrier, NT_DEV - 1 + 2 * NX - 1)

    @pl.loop(1, NT_DEV)
    def _(i):
        k = NT_DEV - i
        send(s.req.at[k], s.got.at[k], s.rsend, s.rrecv.at[lax.div(k, 8)], (at_offset(t, k, 1), g))

    s.place[...] = hot(rel * CAP + rank == iota((SLOTS, TOK), 0))
    loads[2].wait()

    for b in range(4):
        first = 1 if b == 0 else 0
        wait_all(s.got.at[pl.ds(NZ * b + first, NZ - first)], s.rrecv.at[b])
        names = jnp.transpose(s.got[NZ * b : NZ * (b + 1), 0, :].astype(F32))
        col = jnp.concatenate(
            [names[:CAP, j : j + 1] for j in range(NZ)], 0).astype(I32)
        for q in range(4):
            s.onehot[:, 512 * q : 512 * (q + 1)] = hot(col == 512 * q + 1 + iota((24 * NZ, 512), 1))
        rows = dot(s.onehot[...], s.table[...])
        message = rows.reshape(NZ, CAP, D).astype(BF16)
        s.sbuf[NZ * b : NZ * (b + 1)] = message
        if b == 0:
            s.rbuf[0] = message[0]

        @pl.loop(first, NZ)
        def _(i):
            k = NZ * b + (NZ - 1 + first - i)
            send(s.sbuf.at[k], s.rbuf.at[k], s.dsend, s.drecv, (at_offset(t, k, -1), g))

    ids = s.got[:, 0, :]
    high = lax.shift_right_logical(ids, 6).astype(F32).astype(BF16)
    low = (ids & 63).astype(F32).astype(BF16)

    lane = iota((NT_DEV, SLOTS), 1)
    source = jnp.floor((lane.astype(F32) + 0.5) * (1.0 / CAP)).astype(I32)
    lane = iota((128, SLOTS), 1)
    turn = lane - CAP * jnp.floor((lane.astype(F32) + 0.5) * (1.0 / CAP)).astype(I32)
    pick = hot(iota((128, SLOTS), 0) == turn)
    both = dot(high, pick) * 64.0 + dot(low, pick)
    mine = iota((NT_DEV, SLOTS), 0) == source
    name = jnp.sum(jnp.where(mine, both, 0.0), 0, keepdims=True).astype(I32)

    @pl.loop(0, 8)
    def _(i):
        s.hot[block(i, 256), :] = hot(name == i * 256 + 1 + iota((256, SLOTS), 0))

    ends = []
    total = jnp.int32(0)
    for k in range(8):
        total = total + len_ref[0, k]
        ends.append(total)
    for r in range(4):
        pos = 128 * r + iota((128, 128), 0)
        start = jnp.zeros((128, 128), I32)
        for e in ends:
            start = jnp.where(pos >= e, e, start)
        for q in range(4):
            col = 128 * q + iota((128, 128), 1)
            ok = (col >= start) & (col <= pos)
            s.mask[128 * r : 128 * (r + 1), 128 * q : 128 * (q + 1)] = jnp.where(ok, 1.0, 0.0)

    loads[3].wait()
    loads[4].wait()

    @pl.loop(0, 4)
    def _(r):
        rows = block(r, 128)
        s.gmix[rows, :] = dot(s.cot[rows, :], s.w_out[...], NT).astype(BF16).astype(F32)

    lane = iota((D, D), 1)
    source = ((lane >> 1) & 31) * 16 + (lane >> 6) * 2 + (lane & 1)
    s.order[...] = hot(iota((D, D), 0) == source)
    loads[5].wait()
    loads[6].wait()

    @pl.loop(0, 8)
    def _(q):
        s.w_in_t[block(q, 256), :] = jnp.transpose(s.w_in[:, block(q, 256)])

    rest = pl.ds(1, NT_DEV - 1)
    wait_all(s.rbuf.at[rest], s.drecv)
    s.emb[...] = dot(s.place[...], s.rbuf[...].reshape(SLOTS, D), TN).astype(BF16)

    @pl.loop(0, 8)
    def _(q):
        cols = block(q, 256)
        pre = dot(s.emb[...], s.w_in[:, cols])
        sig = 0.5 + 0.5 * jnp.tanh(0.5 * pre)
        act = pre * sig
        s.proj[:, cols] = act.astype(BF16)
        s.slope[:, cols] = sig + act * (1.0 - sig)

    @pl.loop(0, 4)
    def _(p):
        off = pl.multiple_of(p * 128, 128)
        for r in range(2):
            rows = pl.ds(256 * r, 256)
            cols = pl.ds(0, 256 * (r + 1))
            key = s.proj[cols, pl.ds(1536 + off, 128)]
            val = s.proj[cols, pl.ds(512 + off, 128)]
            qry = s.proj[rows, pl.ds(1024 + off, 128)] * jnp.asarray(0.0625, BF16)
            mask = s.mask[rows, cols]
            acc = None
            for half in range(2):
                h = dot(half_lanes(qry, half), key, NT)
                th = jnp.tanh(h)
                um = (1.0 + th) * mask
                w = h * um
                s.d[2 * p + half, rows, cols] = um + w * (1.0 - th)
                wb = w.astype(BF16)
                s.w[2 * p + half, rows, cols] = wb
                some = dot(wb, half_lanes(val, half))
                acc = some if acc is None else acc + some
            s.att[rows, pl.ds(off, 128)] = acc

    s.ggain[...] = jnp.zeros_like(s.ggain)

    @pl.loop(0, 4)
    def _(r):
        rows = block(r, 128)
        att = s.att[rows, :]
        cen = att - jnp.mean(att, 1, keepdims=True)
        inv = lax.rsqrt(jnp.mean(cen * cen, 1, keepdims=True) + 1e-05)
        normed = cen * inv
        gain = s.gain[...]
        upd = s.proj[rows, pl.ds(0, 512)].astype(F32)
        s.mixed[rows, :] = (normed * gain * upd).astype(BF16)
        gmix = s.gmix[rows, :]
        gn = gmix * normed
        s.gpre[rows, pl.ds(0, 512)] = (gn * gain * s.slope[rows, pl.ds(0, 512)]).astype(BF16)
        s.ggain[...] += jnp.sum(gn * upd, 0, keepdims=True)
        gnorm = gmix * gain * upd
        m1 = jnp.mean(gnorm, 1, keepdims=True)
        m2 = jnp.mean(gnorm * normed, 1, keepdims=True)
        s.gatt[rows, :] = ((gnorm - m1 - normed * m2) * inv).astype(BF16)

    mixed = dot(s.mixed[...], s.order[...]).astype(BF16)
    s.gwout[...] = dot(mixed, s.cot[...], TN).astype(BF16)
    s.gx_r[0] = s.ggain[...]

    @pl.loop(0, NX)
    def _(dx):
        send(s.gwout.at[block(x_of(dx) * 2 + other, 64), :], s.oc_r.at[dx], s.ocs, s.ocr, partner)

    @pl.loop(1, 2 * NX)
    def _(k):
        send(s.ggain, s.gx_r.at[k], s.gxs, s.gxr, (t, lax.rem(g + k, 2 * NX)))

    def back_pair(p):
        off = pl.multiple_of(p * 128, 128)
        for r in range(2):
            rows = pl.ds(256 * r, 256)
            cols = pl.ds(0, 256 * (r + 1))
            key = s.proj[cols, pl.ds(1536 + off, 128)] * jnp.asarray(0.0625, BF16)
            val = s.proj[cols, pl.ds(512 + off, 128)]
            qry = s.proj[rows, pl.ds(1024 + off, 128)] * jnp.asarray(0.0625, BF16)
            gat = s.gatt[rows, pl.ds(off, 128)]
            gq = gk = gv = None
            for half in range(2):
                gath = half_lanes(gat, half)
                gw = dot(gath, val, NT)
                gs = (gw * s.d[2 * p + half, rows, cols]).astype(BF16)
                a = dot(gs, half_lanes(key, half))
                b = dot(gs, half_lanes(qry, half), TN)
                v = dot(s.w[2 * p + half, rows, cols], gath, TN)
                gq = a if gq is None else gq + a
                gk = b if gk is None else gk + b
                gv = v if gv is None else gv + v
            qcols = pl.ds(1024 + off, 128)
            s.gpre[rows, qcols] = (gq * s.slope[rows, qcols]).astype(BF16)
            if r == 0:
                s.gacc[0] = gk
                s.gacc[1] = gv
            else:
                for n, acc in ((0, gk), (1, gv)):
                    dst = pl.ds((1536 if n == 0 else 512) + off, 128)
                    for half in range(2):
                        here = pl.ds(256 * half, 256)
                        v = acc[256 * half : 256 * (half + 1)]
                        v = v + s.gacc[n] if half == 0 else v
                        s.gpre[here, dst] = (v * s.slope[here, dst]).astype(BF16)

    pl.loop(0, 2)(back_pair)
    wait_all(s.oc_r, s.ocr)
    for dx in FAR_X + (0,):
        o = s.gwout[block(x_of(dx) * 2 + c, 64), :].astype(F32) + s.oc_r[dx].astype(F32)
        if dx:
            s.ox_s[dx] = o.astype(BF16)
            send(s.ox_s.at[dx], s.ox_r.at[dx], s.oxs, s.oxr, (t, x_of(dx) * 2 + c))
        else:
            s.ox_own[...] = o
    pl.loop(2, 4)(back_pair)

    @pl.loop(0, 2)
    def _(q):
        cols = block(q, 256)
        v = dot(s.gpre[...], s.w_in_t[:, cols])
        s.gemb[:, cols] = (s.cot[:, cols].astype(F32) + v).astype(BF16)

    rest_x, rest_y, rest_z = pl.ds(1, NX - 1), pl.ds(1, NY - 1), pl.ds(1, NZ - 1)
    rest_g = pl.ds(1, 2 * NX - 1)

    def outer_y():
        wait_all(s.ox_r.at[rest_x], s.oxr)
        wait_all(s.gx_r.at[rest_g], s.gxr)
        o = s.ox_own[...] + s.ox_r[1].astype(F32) + s.ox_r[2].astype(F32) + s.ox_r[3].astype(F32)
        s.oy_own[...] = o.reshape(NY, 16, D)
        s.oy_s[...] = o.astype(BF16).reshape(NY, 16, D)
        s.gy_s[...] = jnp.sum(s.gx_r[...], 0)
        s.gy_r[0] = s.gy_s[...]

        @pl.loop(1, NY)
        def _(k):
            yy = lax.rem(y + k, NY)
            to = (yy * NZ + z, g)
            send(s.oy_s.at[yy], s.oy_r.at[k], s.wys.at[1], s.wyr.at[1], to)
            send(s.gy_s, s.gy_r.at[k], s.wys.at[2], s.wyr.at[2], to)

    def outer_z():
        wait_all(s.oy_r.at[rest_y], s.wyr.at[1])
        wait_all(s.gy_r.at[rest_y], s.wyr.at[2])
        o = s.oy_own[y] + s.oy_r[1].astype(F32) + s.oy_r[2].astype(F32) + s.oy_r[3].astype(F32)
        for k in range(NZ):
            s.oz_s[k] = o[2 * k : 2 * k + 2]
        s.gz_s[...] = jnp.sum(s.gy_r[...], 0)
        s.gz_r[0] = s.gz_s[...]
        s.oz_r[0] = s.oz_s[z]

        @pl.loop(1, NZ)
        def _(k):
            zz = lax.rem(z + k, NZ)
            to = (y * NZ + zz, g)
            send(s.oz_s.at[zz], s.oz_r.at[k], s.wzs.at[1], s.wzr.at[1], to)
            send(s.gz_s, s.gz_r.at[k], s.wzs.at[2], s.wzr.at[2], to)

    def outer_g():
        wait_all(s.oz_r.at[rest_z], s.wzr.at[1])
        s.og_s[...] = jnp.sum(s.oz_r[...], 0)
        s.og_r[0] = s.og_s[...]

        @pl.loop(1, 2 * NX)
        def _(k):
            send(s.og_s, s.og_r.at[k], s.ogs, s.ogr, (t, lax.rem(g + k, 2 * NX)))

        wait_all(s.gz_r.at[rest_z], s.wzr.at[2])
        total = jnp.sum(s.gz_r[...], 0)
        pick = jnp.where(iota((D, 128), 0) == 16 * t + iota((D, 128), 1), 1.0, 0.0)
        gaing_ref[...] = lax.dot_general(
            jnp.broadcast_to(total, (8, D)), pick, NN,
            precision=lax.Precision.HIGHEST, preferred_element_type=F32)[:1]

    def inner_core():
        s.emb_t[...] = jnp.transpose(s.emb[...])
        for dx in FAR_X + (0,):
            cols = block(x_of(dx) * 2 + other, 256)
            s.wc_s[dx] = dot(s.emb_t[...], s.gpre[:, cols]).astype(BF16)
            send(s.wc_s.at[dx], s.wc_r.at[dx], s.wcs.at[dx], s.wcr.at[dx], partner)
        for dx in FAR_X + (0,):
            w = dot(s.emb_t[...], s.gpre[:, block(x_of(dx) * 2 + c, 256)])
            wait_all(s.wc_r.at[dx], s.wcr.at[dx])
            w = w + s.wc_r[dx].astype(F32)
            if dx == 2:
                for n, to in ((0, 1), (1, 3)):
                    s.wh_s[n] = w[256 * n : 256 * (n + 1)].astype(BF16)
                    send(s.wh_s.at[n], s.wh_r.at[n], s.whs.at[n], s.whr.at[n],
                         (t, x_of(to) * 2 + c))
            else:
                s.wf[dx] = w

    def inner_x():
        for n, dx in ((0, 1), (1, 3)):
            wait_all(s.wh_r.at[n], s.whr.at[n])
            near, far = pl.ds(256 * n, 256), pl.ds(256 * (1 - n), 256)
            s.wx_s[dx, near, :] = (s.wf[dx, near, :] + s.wh_r[n].astype(F32)).astype(BF16)
            s.wx_s[dx, far, :] = s.wf[dx, far, :].astype(BF16)
            send(s.wx_s.at[dx], s.wx_r.at[dx], s.wxs.at[dx], s.wxr.at[dx], (t, x_of(dx) * 2 + c))

    def inner_y():
        wait_all(s.wx_r.at[1], s.wxr.at[1])
        wait_all(s.wx_r.at[3], s.wxr.at[3])
        w = s.wf[0] + s.wx_r[1].astype(F32) + s.wx_r[3].astype(F32)
        s.wy_own[...] = w.reshape(NY, 128, 256)
        s.wy_s[...] = w.astype(BF16).reshape(NY, 128, 256)

        @pl.loop(1, NY)
        def _(k):
            yy = lax.rem(y + k, NY)
            send(s.wy_s.at[yy], s.wy_r.at[k], s.wys.at[0], s.wyr.at[0], (yy * NZ + z, g))

    def inner_z():
        wait_all(s.wy_r.at[rest_y], s.wyr.at[0])
        w = s.wy_own[y] + s.wy_r[1].astype(F32) + s.wy_r[2].astype(F32) + s.wy_r[3].astype(F32)
        s.wz_own[...] = w.reshape(NZ, 16, 256)
        s.wz_s[...] = w.astype(BF16).reshape(NZ, 16, 256)

        @pl.loop(1, NZ)
        def _(k):
            zz = lax.rem(z + k, NZ)
            send(s.wz_s.at[zz], s.wz_r.at[k], s.wzs.at[0], s.wzr.at[0], (y * NZ + zz, g))

    def table_send(h):
        ibuf, tc_s, tc_r = part("ibuf", h), part("tc_s", h), part("tc_r", h)
        tx_s, tx_r = part("tx_s", h), part("tx_r", h)
        wait_all(ibuf.at[rest], s.isem.at[h])

        def table_rows(which):
            return dot(s.hot[block(which, 256), :], ibuf[...].reshape(SLOTS, WIDTHS[h]))

        for dx in FAR_X + (0,):
            tc_s[dx] = table_rows(x_of(dx) * 2 + other).astype(BF16)
            send(tc_s.at[dx], tc_r.at[dx], s.tcs.at[h, dx], s.tcr.at[h, dx], partner)
        for dx in FAR_X + (0,):
            own = table_rows(x_of(dx) * 2 + c)
            wait_all(tc_r.at[dx], s.tcr.at[h, dx])
            own = own + tc_r[dx].astype(F32)
            if dx:
                tx_s[dx] = own.astype(BF16)
                send(tx_s.at[dx], tx_r.at[dx], s.txs.at[h], s.txr.at[h], (t, x_of(dx) * 2 + c))
            else:
                part("tx_own", h)[...] = own

    def table_finish(h):
        tx_r = part("tx_r", h)
        wait_all(tx_r.at[rest_x], s.txr.at[h])
        tgrad_ref[:, STARTS[h] : STARTS[h] + WIDTHS[h]] = (
            part("tx_own", h)[...] + tx_r[1].astype(F32) + tx_r[2].astype(F32) + tx_r[3].astype(F32))

    outer_y()

    for n in range(2):
        out = dot(s.place[...], s.gemb[:, 256 * n : 256 * (n + 1)])
        for h in ((0,), (1, 2))[n]:
            lo = STARTS[h] - 256 * n
            message = out[:, lo : lo + WIDTHS[h]].reshape(NT_DEV, CAP, WIDTHS[h]).astype(BF16)
            obuf, ibuf = part("obuf", h), part("ibuf", h)
            obuf[...] = message
            ibuf[0] = message[0]

            @pl.loop(1, NT_DEV)
            def _(i):
                k = NT_DEV - i
                send(obuf.at[k], ibuf.at[k], s.ssem.at[h], s.isem.at[h], (at_offset(t, k, 1), g))

    inner_core()

    @pl.loop(0, 4)
    def _(r):
        rows = block(r, 128)
        out = dot(s.mixed[rows, :], s.w_out[...])
        res_ref[rows, :] = (s.emb[rows, :].astype(F32) + out).astype(BF16)

    inner_x()
    table_send(0)
    inner_y()
    table_send(1)
    outer_z()
    table_send(2)
    inner_z()
    outer_g()
    table_finish(0)
    table_finish(1)
    wait_all(s.wz_r.at[rest_z], s.wzr.at[0])
    wing_ref[...] = s.wz_own[z] + jnp.sum(s.wz_r[1:].astype(F32), 0)
    wait_all(s.og_r.at[rest_g], s.ogr)
    woutg_ref[...] = jnp.concatenate([s.og_r[lax.rem(g + 2 * NX - k, 2 * NX)] for k in range(2 * NX)], 0)
    table_finish(2)

    wait_all(s.req.at[rest], s.rsend)
    wait_all(s.sbuf.at[rest], s.dsend)
    for h in range(CHUNKS):
        wait_all(part("obuf", h).at[rest], s.ssem.at[h])
        wait_all(part("tx_s", h).at[rest_x], s.txs.at[h])
        for dx in range(NX):
            wait_all(part("tc_s", h).at[dx], s.tcs.at[h, dx])
    for dx in range(NX):
        wait_all(s.wc_s.at[dx], s.wcs.at[dx])
    wait_all(s.oc_r, s.ocs)
    wait_all(s.gx_r.at[rest_g], s.gxs)
    for n, dx in ((0, 1), (1, 3)):
        wait_all(s.wh_s.at[n], s.whs.at[n])
        wait_all(s.wx_s.at[dx], s.wxs.at[dx])
    wait_all(s.ox_s.at[rest_x], s.oxs)
    wait_all(s.wy_s.at[rest_y], s.wys.at[0])
    wait_all(s.oy_s.at[rest_y], s.wys.at[1])
    wait_all(s.gy_r.at[rest_y], s.wys.at[2])
    wait_all(s.wz_s.at[rest_z], s.wzs.at[0])
    wait_all(s.oz_s.at[rest_z], s.wzs.at[1])
    wait_all(s.gz_r.at[rest_z], s.wzs.at[2])
    wait_all(s.og_r.at[rest_g], s.ogs)


def finish_kernel(res, tgrad, wing, woutg, gaing, res_o, tgrad_o, wing_o, woutg_o, gaing_o):
    res_o[...] = res[...]
    tgrad_o[...] = tgrad[...]
    wing_o[...] = wing[...]
    woutg_o[...] = woutg[...]
    gaing_o[...] = gaing[:, :16]


def on_device(item_owner, item_row, lengths, table, w_in, w_out, gain, cotangent):
    vm = pl.BlockSpec(memory_space=pltpu.VMEM)
    hbm = pl.BlockSpec(memory_space=pltpu.HBM)
    shapes = (
        jax.ShapeDtypeStruct((TOK, D), BF16),
        jax.ShapeDtypeStruct((256, D), F32),
        jax.ShapeDtypeStruct((16, 256), F32),
        jax.ShapeDtypeStruct((16, D), F32),
    )
    outs = pl.pallas_call(
        kernel,
        name="whole",
        out_shape=shapes + (jax.ShapeDtypeStruct((1, 128), F32),),
        in_specs=[pl.BlockSpec(memory_space=pltpu.SMEM)] + [hbm] * 7,
        out_specs=[vm] * 5,
        scratch_shapes=list(scratch().values()),
        compiler_params=pltpu.CompilerParams(
            collective_id=1, has_side_effects=True, vmem_limit_bytes=60 * 2**20
        ),
    )(lengths, item_owner.reshape(1, TOK), item_row.reshape(1, TOK), table, w_in, w_out,
      gain.reshape(1, D), cotangent)
    res, tgrad, wing, woutg, gaing = pl.pallas_call(
        finish_kernel,
        name="finish",
        out_shape=shapes + (jax.ShapeDtypeStruct((1, 16), F32),),
        in_specs=[vm] * 5,
        out_specs=[vm] * 5,
    )(*outs)
    return res, tgrad, wing, woutg, gaing.reshape(16)


def solution(mesh):
    return jax.shard_map(
        on_device,
        mesh=mesh,
        in_specs=(
            P(("table", "group"), None),
            P(("table", "group")),
            P(("table", "group"), None),
            P("table", None),
            P(),
            P(),
            P(),
            P(("table", "group"), None),
        ),
        out_specs=(
            P(("table", "group"), None),
            P(("table", "group"), None),
            P("table", "group"),
            P("table", None),
            P("table"),
        ),
        check_vma=False,
    )
```

```python
import types

import jax
import jax.numpy as jnp
from jax import lax
from jax.experimental import pallas as pl
from jax.experimental.pallas import tpu as pltpu
from jax.sharding import PartitionSpec as P

D = 512
TOK = 512
NY, NZ, NX = 4, 8, 4
NT_DEV = NY * NZ
CAP = 24
SLOTS = CAP * NT_DEV
WIDTHS = (256, 128, 128)
STARTS = (0, 256, 384)
CHUNKS = len(WIDTHS)
F32 = jnp.float32
BF16 = jnp.bfloat16
I32 = jnp.int32
NT = (((1,), (1,)), ((), ()))
TN = (((0,), (0,)), ((), ()))
NN = (((1,), (0,)), ((), ()))
MESH = pl.DeviceIdType.MESH
FAR_X = (2, 1, 3)


def dot(a, b, dims=NN):
    return lax.dot_general(a, b, dims, preferred_element_type=F32)


def iota(shape, axis):
    return lax.broadcasted_iota(I32, shape, axis)


def hot(cond):
    return jnp.where(cond, 1.0, 0.0).astype(BF16)


def half_lanes(v, half):
    lane = iota(v.shape, 1)
    keep = (lane < 64) if half == 0 else (lane >= 64)
    return jnp.where(keep, v, jnp.zeros_like(v))


def at_offset(t, k, sign):
    y, z = lax.div(t, NZ), lax.rem(t, NZ)
    step, dy = lax.div(k, NY), lax.rem(k, NY)
    half = lax.div(step + 1, 2)
    dz = jnp.where(lax.rem(step, 2) == 1, half, NZ - half)
    yy = lax.rem(y + sign * dy + NY, NY)
    zz = lax.rem(z + sign * dz + NZ, NZ)
    return yy * NZ + zz


def wait_all(ref, sem):
    pltpu.make_async_copy(ref, ref, sem).wait()


def send(src, dst, send_sem, recv_sem, to):
    pltpu.make_async_remote_copy(
        src_ref=src, dst_ref=dst, send_sem=send_sem, recv_sem=recv_sem,
        device_id=to, device_id_type=MESH,
    ).start()


def block(i, size):
    return pl.ds(pl.multiple_of(i * size, size), size)


def scratch():
    vm = pltpu.VMEM
    dma = pltpu.SemaphoreType.DMA
    return dict(
        own=vm((1, TOK), I32), row=vm((1, TOK), I32), table=vm((2048, D), BF16),
        w_in=vm((D, 2048), BF16), w_out=vm((D, D), BF16), cot=vm((TOK, D), BF16),
        gain=vm((1, D), F32),
        req=vm((NT_DEV, 1, 128), I32), got=vm((NT_DEV, 1, 128), I32),
        onehot=vm((24 * NZ, 2048), BF16), sbuf=vm((NT_DEV, CAP, D), BF16),
        rbuf=vm((NT_DEV, CAP, D), BF16), place=vm((SLOTS, TOK), BF16),
        hot=vm((2048, SLOTS), BF16),
        emb=vm((TOK, D), BF16), emb_t=vm((D, TOK), BF16), w_in_t=vm((2048, D), BF16),
        slope=vm((TOK, 2048), F32), proj=vm((TOK, 2048), BF16), w=vm((8, TOK, TOK), BF16),
        d=vm((8, TOK, TOK), F32), mask=vm((TOK, TOK), F32), att=vm((TOK, D), F32),
        gmix=vm((TOK, D), F32), gatt=vm((TOK, D), BF16), gpre=vm((TOK, 2048), BF16),
        mixed=vm((TOK, D), BF16), gacc=vm((2, 256, 128), F32), gemb=vm((TOK, D), BF16),
        order=vm((D, D), BF16), gwout=vm((D, D), BF16), ggain=vm((1, D), F32),
        **{f"obuf{h}": vm((NT_DEV, CAP, w), BF16) for h, w in enumerate(WIDTHS)},
        **{f"ibuf{h}": vm((NT_DEV, CAP, w), BF16) for h, w in enumerate(WIDTHS)},
        **{f"{n}{h}": vm((NX, 256, w), BF16) for h, w in enumerate(WIDTHS)
           for n in ("tc_s", "tc_r", "tx_s", "tx_r")},
        **{f"tx_own{h}": vm((256, w), F32) for h, w in enumerate(WIDTHS)},
        wc_s=vm((NX, D, 256), BF16), wc_r=vm((NX, D, 256), BF16), oc_r=vm((NX, 64, D), BF16),
        wx_s=vm((NX, D, 256), BF16), wx_r=vm((NX, D, 256), BF16), wf=vm((NX, D, 256), F32), wh_s=vm((2, 256, 256), BF16), wh_r=vm((2, 256, 256), BF16),
        ox_s=vm((NX, 64, D), BF16), ox_r=vm((NX, 64, D), BF16), ox_own=vm((64, D), F32),
        gx_r=vm((2 * NX, 1, D), F32),
        wy_s=vm((NY, 128, 256), BF16), wy_r=vm((NY, 128, 256), BF16), wy_own=vm((NY, 128, 256), F32),
        oy_s=vm((NY, 16, D), BF16), oy_r=vm((NY, 16, D), BF16), oy_own=vm((NY, 16, D), F32),
        gy_s=vm((1, D), F32), gy_r=vm((NY, 1, D), F32),
        wz_s=vm((NZ, 16, 256), BF16), wz_r=vm((NZ, 16, 256), BF16), wz_own=vm((NZ, 16, 256), F32),
        oz_s=vm((NZ, 2, D), F32), oz_r=vm((NZ, 2, D), F32),
        gz_s=vm((1, D), F32), gz_r=vm((NZ, 1, D), F32),
        og_s=vm((2, D), F32), og_r=vm((2 * NX, 2, D), F32),
        load=dma((7,)), rsend=dma, rrecv=dma((NY,)), dsend=dma, drecv=dma,
        ssem=dma((CHUNKS,)), isem=dma((CHUNKS,)),
        tcs=dma((CHUNKS, NX)), tcr=dma((CHUNKS, NX)), txs=dma((CHUNKS,)), txr=dma((CHUNKS,)),
        wcs=dma((NX,)), wcr=dma((NX,)), ocs=dma, ocr=dma, gxs=dma, gxr=dma,
        wxs=dma((NX,)), wxr=dma((NX,)), whs=dma((2,)), whr=dma((2,)), oxs=dma, oxr=dma, wys=dma((3,)), wyr=dma((3,)), wzs=dma((3,)), wzr=dma((3,)),
        ogs=dma, ogr=dma,
    )


def kernel(len_ref, own_h, row_h, table_h, w_in_h, w_out_h, gain_h, cot_h,
           res_ref, tgrad_ref, wing_ref, woutg_ref, gaing_ref, *refs):
    s = types.SimpleNamespace(**dict(zip(scratch(), refs)))

    def part(name, h):
        return getattr(s, name + str(h))

    t, g = lax.axis_index("table"), lax.axis_index("group")
    x, c = lax.div(g, 2), lax.rem(g, 2)
    other = 1 - c
    y, z = lax.div(t, NZ), lax.rem(t, NZ)
    partner = (t, x * 2 + other)
    barrier = pltpu.get_barrier_semaphore()

    loads = [
        pltpu.make_async_copy(src, dst, s.load.at[i])
        for i, (src, dst) in enumerate((
            (own_h, s.own), (row_h, s.row), (table_h, s.table), (w_out_h, s.w_out),
            (cot_h, s.cot), (w_in_h, s.w_in), (gain_h, s.gain)))
    ]
    for copy in loads:
        copy.start()

    @pl.loop(1, NT_DEV)
    def _(k):
        pl.semaphore_signal(
            barrier, inc=1, device_id=(at_offset(t, NT_DEV - k, 1), g), device_id_type=MESH)

    @pl.loop(1, 2 * NX)
    def _(k):
        pl.semaphore_signal(
            barrier, inc=1, device_id=(t, lax.rem(g + k, 2 * NX)), device_id_type=MESH)

    def x_of(dx):
        return lax.rem(x + dx, NX)

    loads[0].wait()
    loads[1].wait()
    own = s.own[...]
    dy = (lax.shift_right_logical(own, 3) - y) & (NY - 1)
    dz = ((own & (NZ - 1)) - z) & (NZ - 1)
    step = jnp.where(dz == 0, 0, jnp.where(dz <= NZ // 2, 2 * dz - 1, 2 * (NZ - dz)))
    rel = step * NY + dy
    is_rel = rel == iota((NT_DEV, TOK), 0)
    before = dot(hot(is_rel), hot(iota((TOK, TOK), 0) < iota((TOK, TOK), 1)))
    rank = jnp.sum(jnp.where(is_rel, before, 0.0), 0, keepdims=True).astype(I32)
    idx = s.row[...] + 1
    ranks = hot(rank == iota((128, TOK), 0))
    high = jnp.where(is_rel, lax.shift_right_logical(idx, 6).astype(F32), 0.0).astype(BF16)
    low = jnp.where(is_rel, (idx & 63).astype(F32), 0.0).astype(BF16)
    wanted = dot(high, ranks, NT) * 64.0 + dot(low, ranks, NT)
    s.req[...] = wanted.astype(I32).reshape(NT_DEV, 1, 128)
    s.got[0] = s.req[0]

    pl.semaphore_wait(barrier, NT_DEV - 1 + 2 * NX - 1)

    @pl.loop(1, NT_DEV)
    def _(i):
        k = NT_DEV - i
        send(s.req.at[k], s.got.at[k], s.rsend, s.rrecv.at[lax.div(k, 8)], (at_offset(t, k, 1), g))

    s.place[...] = hot(rel * CAP + rank == iota((SLOTS, TOK), 0))
    loads[2].wait()

    for b in range(4):
        first = 1 if b == 0 else 0
        wait_all(s.got.at[pl.ds(NZ * b + first, NZ - first)], s.rrecv.at[b])
        names = jnp.transpose(s.got[NZ * b : NZ * (b + 1), 0, :].astype(F32))
        col = jnp.concatenate(
            [names[:CAP, j : j + 1] for j in range(NZ)], 0).astype(I32)
        for q in range(4):
            s.onehot[:, 512 * q : 512 * (q + 1)] = hot(col == 512 * q + 1 + iota((24 * NZ, 512), 1))
        rows = dot(s.onehot[...], s.table[...])
        message = rows.reshape(NZ, CAP, D).astype(BF16)
        s.sbuf[NZ * b : NZ * (b + 1)] = message
        if b == 0:
            s.rbuf[0] = message[0]

        @pl.loop(first, NZ)
        def _(i):
            k = NZ * b + (NZ - 1 + first - i)
            send(s.sbuf.at[k], s.rbuf.at[k], s.dsend, s.drecv, (at_offset(t, k, -1), g))

    ids = s.got[:, 0, :]
    high = lax.shift_right_logical(ids, 6).astype(F32).astype(BF16)
    low = (ids & 63).astype(F32).astype(BF16)

    lane = iota((NT_DEV, SLOTS), 1)
    source = jnp.floor((lane.astype(F32) + 0.5) * (1.0 / CAP)).astype(I32)
    lane = iota((128, SLOTS), 1)
    turn = lane - CAP * jnp.floor((lane.astype(F32) + 0.5) * (1.0 / CAP)).astype(I32)
    pick = hot(iota((128, SLOTS), 0) == turn)
    both = dot(high, pick) * 64.0 + dot(low, pick)
    mine = iota((NT_DEV, SLOTS), 0) == source
    name = jnp.sum(jnp.where(mine, both, 0.0), 0, keepdims=True).astype(I32)

    @pl.loop(0, 8)
    def _(i):
        s.hot[block(i, 256), :] = hot(name == i * 256 + 1 + iota((256, SLOTS), 0))

    ends = []
    total = jnp.int32(0)
    for k in range(8):
        total = total + len_ref[0, k]
        ends.append(total)
    for r in range(4):
        pos = 128 * r + iota((128, 128), 0)
        start = jnp.zeros((128, 128), I32)
        for e in ends:
            start = jnp.where(pos >= e, e, start)
        for q in range(4):
            col = 128 * q + iota((128, 128), 1)
            ok = (col >= start) & (col <= pos)
            s.mask[128 * r : 128 * (r + 1), 128 * q : 128 * (q + 1)] = jnp.where(ok, 1.0, 0.0)

    loads[3].wait()
    loads[4].wait()

    @pl.loop(0, 4)
    def _(r):
        rows = block(r, 128)
        s.gmix[rows, :] = dot(s.cot[rows, :], s.w_out[...], NT).astype(BF16).astype(F32)

    lane = iota((D, D), 1)
    source = ((lane >> 1) & 31) * 16 + (lane >> 6) * 2 + (lane & 1)
    s.order[...] = hot(iota((D, D), 0) == source)
    loads[5].wait()
    loads[6].wait()

    @pl.loop(0, 8)
    def _(q):
        s.w_in_t[block(q, 256), :] = jnp.transpose(s.w_in[:, block(q, 256)])

    rest = pl.ds(1, NT_DEV - 1)
    wait_all(s.rbuf.at[rest], s.drecv)
    s.emb[...] = dot(s.place[...], s.rbuf[...].reshape(SLOTS, D), TN).astype(BF16)

    @pl.loop(0, 8, unroll=4)
    def _(q):
        cols = block(q, 256)
        pre = dot(s.emb[...], s.w_in[:, cols])
        sig = 0.5 + 0.5 * jnp.tanh(0.5 * pre)
        act = pre * sig
        s.proj[:, cols] = act.astype(BF16)
        s.slope[:, cols] = sig + act * (1.0 - sig)

    @pl.loop(0, 4, unroll=4)
    def _(p):
        off = pl.multiple_of(p * 128, 128)
        for r in range(2):
            rows = pl.ds(256 * r, 256)
            cols = pl.ds(0, 256 * (r + 1))
            key = s.proj[cols, pl.ds(1536 + off, 128)]
            val = s.proj[cols, pl.ds(512 + off, 128)]
            qry = s.proj[rows, pl.ds(1024 + off, 128)] * jnp.asarray(0.0625, BF16)
            mask = s.mask[rows, cols]
            acc = None
            for half in range(2):
                h = dot(half_lanes(qry, half), key, NT)
                th = jnp.tanh(h)
                um = (1.0 + th) * mask
                w = h * um
                s.d[2 * p + half, rows, cols] = um + w * (1.0 - th)
                wb = w.astype(BF16)
                s.w[2 * p + half, rows, cols] = wb
                some = dot(wb, half_lanes(val, half))
                acc = some if acc is None else acc + some
            s.att[rows, pl.ds(off, 128)] = acc

    s.ggain[...] = jnp.zeros_like(s.ggain)

    @pl.loop(0, 4, unroll=2)
    def _(r):
        rows = block(r, 128)
        att = s.att[rows, :]
        cen = att - jnp.mean(att, 1, keepdims=True)
        inv = lax.rsqrt(jnp.mean(cen * cen, 1, keepdims=True) + 1e-05)
        normed = cen * inv
        gain = s.gain[...]
        upd = s.proj[rows, pl.ds(0, 512)].astype(F32)
        s.mixed[rows, :] = (normed * gain * upd).astype(BF16)
        gmix = s.gmix[rows, :]
        gn = gmix * normed
        s.gpre[rows, pl.ds(0, 512)] = (gn * gain * s.slope[rows, pl.ds(0, 512)]).astype(BF16)
        s.ggain[...] += jnp.sum(gn * upd, 0, keepdims=True)
        gnorm = gmix * gain * upd
        m1 = jnp.mean(gnorm, 1, keepdims=True)
        m2 = jnp.mean(gnorm * normed, 1, keepdims=True)
        s.gatt[rows, :] = ((gnorm - m1 - normed * m2) * inv).astype(BF16)

    mixed = dot(s.mixed[...], s.order[...]).astype(BF16)
    s.gwout[...] = dot(mixed, s.cot[...], TN).astype(BF16)
    s.gx_r[0] = s.ggain[...]

    @pl.loop(0, NX)
    def _(dx):
        send(s.gwout.at[block(x_of(dx) * 2 + other, 64), :], s.oc_r.at[dx], s.ocs, s.ocr, partner)

    @pl.loop(1, 2 * NX)
    def _(k):
        send(s.ggain, s.gx_r.at[k], s.gxs, s.gxr, (t, lax.rem(g + k, 2 * NX)))

    def back_pair(p):
        off = pl.multiple_of(p * 128, 128)
        for r in range(2):
            rows = pl.ds(256 * r, 256)
            cols = pl.ds(0, 256 * (r + 1))
            key = s.proj[cols, pl.ds(1536 + off, 128)] * jnp.asarray(0.0625, BF16)
            val = s.proj[cols, pl.ds(512 + off, 128)]
            qry = s.proj[rows, pl.ds(1024 + off, 128)] * jnp.asarray(0.0625, BF16)
            gat = s.gatt[rows, pl.ds(off, 128)]
            gq = gk = gv = None
            for half in range(2):
                gath = half_lanes(gat, half)
                gw = dot(gath, val, NT)
                gs = (gw * s.d[2 * p + half, rows, cols]).astype(BF16)
                a = dot(gs, half_lanes(key, half))
                b = dot(gs, half_lanes(qry, half), TN)
                v = dot(s.w[2 * p + half, rows, cols], gath, TN)
                gq = a if gq is None else gq + a
                gk = b if gk is None else gk + b
                gv = v if gv is None else gv + v
            qcols = pl.ds(1024 + off, 128)
            s.gpre[rows, qcols] = (gq * s.slope[rows, qcols]).astype(BF16)
            if r == 0:
                s.gacc[0] = gk
                s.gacc[1] = gv
            else:
                for n, acc in ((0, gk), (1, gv)):
                    dst = pl.ds((1536 if n == 0 else 512) + off, 128)
                    for half in range(2):
                        here = pl.ds(256 * half, 256)
                        v = acc[256 * half : 256 * (half + 1)]
                        v = v + s.gacc[n] if half == 0 else v
                        s.gpre[here, dst] = (v * s.slope[here, dst]).astype(BF16)

    pl.loop(0, 2, unroll=2)(back_pair)
    wait_all(s.oc_r, s.ocr)
    for dx in FAR_X + (0,):
        o = s.gwout[block(x_of(dx) * 2 + c, 64), :].astype(F32) + s.oc_r[dx].astype(F32)
        if dx:
            s.ox_s[dx] = o.astype(BF16)
            send(s.ox_s.at[dx], s.ox_r.at[dx], s.oxs, s.oxr, (t, x_of(dx) * 2 + c))
        else:
            s.ox_own[...] = o
    pl.loop(2, 4, unroll=2)(back_pair)

    @pl.loop(0, 2, unroll=2)
    def _(q):
        cols = block(q, 256)
        v = dot(s.gpre[...], s.w_in_t[:, cols])
        s.gemb[:, cols] = (s.cot[:, cols].astype(F32) + v).astype(BF16)

    rest_x, rest_y, rest_z = pl.ds(1, NX - 1), pl.ds(1, NY - 1), pl.ds(1, NZ - 1)
    rest_g = pl.ds(1, 2 * NX - 1)

    def outer_y():
        wait_all(s.ox_r.at[rest_x], s.oxr)
        wait_all(s.gx_r.at[rest_g], s.gxr)
        o = s.ox_own[...] + s.ox_r[1].astype(F32) + s.ox_r[2].astype(F32) + s.ox_r[3].astype(F32)
        s.oy_own[...] = o.reshape(NY, 16, D)
        s.oy_s[...] = o.astype(BF16).reshape(NY, 16, D)
        s.gy_s[...] = jnp.sum(s.gx_r[...], 0)
        s.gy_r[0] = s.gy_s[...]

        @pl.loop(1, NY)
        def _(k):
            yy = lax.rem(y + k, NY)
            to = (yy * NZ + z, g)
            send(s.oy_s.at[yy], s.oy_r.at[k], s.wys.at[1], s.wyr.at[1], to)
            send(s.gy_s, s.gy_r.at[k], s.wys.at[2], s.wyr.at[2], to)

    def outer_z():
        wait_all(s.oy_r.at[rest_y], s.wyr.at[1])
        wait_all(s.gy_r.at[rest_y], s.wyr.at[2])
        o = s.oy_own[y] + s.oy_r[1].astype(F32) + s.oy_r[2].astype(F32) + s.oy_r[3].astype(F32)
        for k in range(NZ):
            s.oz_s[k] = o[2 * k : 2 * k + 2]
        s.gz_s[...] = jnp.sum(s.gy_r[...], 0)
        s.gz_r[0] = s.gz_s[...]
        s.oz_r[0] = s.oz_s[z]

        @pl.loop(1, NZ)
        def _(k):
            zz = lax.rem(z + k, NZ)
            to = (y * NZ + zz, g)
            send(s.oz_s.at[zz], s.oz_r.at[k], s.wzs.at[1], s.wzr.at[1], to)
            send(s.gz_s, s.gz_r.at[k], s.wzs.at[2], s.wzr.at[2], to)

    def outer_g():
        wait_all(s.oz_r.at[rest_z], s.wzr.at[1])
        s.og_s[...] = jnp.sum(s.oz_r[...], 0)
        s.og_r[0] = s.og_s[...]

        @pl.loop(1, 2 * NX)
        def _(k):
            send(s.og_s, s.og_r.at[k], s.ogs, s.ogr, (t, lax.rem(g + k, 2 * NX)))

        wait_all(s.gz_r.at[rest_z], s.wzr.at[2])
        total = jnp.sum(s.gz_r[...], 0)
        pick = jnp.where(iota((D, 128), 0) == 16 * t + iota((D, 128), 1), 1.0, 0.0)
        gaing_ref[...] = lax.dot_general(
            jnp.broadcast_to(total, (8, D)), pick, NN,
            precision=lax.Precision.HIGHEST, preferred_element_type=F32)[:1]

    def inner_core():
        s.emb_t[...] = jnp.transpose(s.emb[...])
        for dx in FAR_X + (0,):
            cols = block(x_of(dx) * 2 + other, 256)
            s.wc_s[dx] = dot(s.emb_t[...], s.gpre[:, cols]).astype(BF16)
            send(s.wc_s.at[dx], s.wc_r.at[dx], s.wcs.at[dx], s.wcr.at[dx], partner)
        for dx in FAR_X + (0,):
            w = dot(s.emb_t[...], s.gpre[:, block(x_of(dx) * 2 + c, 256)])
            wait_all(s.wc_r.at[dx], s.wcr.at[dx])
            w = w + s.wc_r[dx].astype(F32)
            if dx == 2:
                for n, to in ((0, 1), (1, 3)):
                    s.wh_s[n] = w[256 * n : 256 * (n + 1)].astype(BF16)
                    send(s.wh_s.at[n], s.wh_r.at[n], s.whs.at[n], s.whr.at[n],
                         (t, x_of(to) * 2 + c))
            else:
                s.wf[dx] = w

    def inner_x():
        for n, dx in ((0, 1), (1, 3)):
            wait_all(s.wh_r.at[n], s.whr.at[n])
            near, far = pl.ds(256 * n, 256), pl.ds(256 * (1 - n), 256)
            s.wx_s[dx, near, :] = (s.wf[dx, near, :] + s.wh_r[n].astype(F32)).astype(BF16)
            s.wx_s[dx, far, :] = s.wf[dx, far, :].astype(BF16)
            send(s.wx_s.at[dx], s.wx_r.at[dx], s.wxs.at[dx], s.wxr.at[dx], (t, x_of(dx) * 2 + c))

    def inner_y():
        wait_all(s.wx_r.at[1], s.wxr.at[1])
        wait_all(s.wx_r.at[3], s.wxr.at[3])
        w = s.wf[0] + s.wx_r[1].astype(F32) + s.wx_r[3].astype(F32)
        s.wy_own[...] = w.reshape(NY, 128, 256)
        s.wy_s[...] = w.astype(BF16).reshape(NY, 128, 256)

        @pl.loop(1, NY)
        def _(k):
            yy = lax.rem(y + k, NY)
            send(s.wy_s.at[yy], s.wy_r.at[k], s.wys.at[0], s.wyr.at[0], (yy * NZ + z, g))

    def inner_z():
        wait_all(s.wy_r.at[rest_y], s.wyr.at[0])
        w = s.wy_own[y] + s.wy_r[1].astype(F32) + s.wy_r[2].astype(F32) + s.wy_r[3].astype(F32)
        s.wz_own[...] = w.reshape(NZ, 16, 256)
        s.wz_s[...] = w.astype(BF16).reshape(NZ, 16, 256)

        @pl.loop(1, NZ)
        def _(k):
            zz = lax.rem(z + k, NZ)
            send(s.wz_s.at[zz], s.wz_r.at[k], s.wzs.at[0], s.wzr.at[0], (y * NZ + zz, g))

    def table_send(h):
        ibuf, tc_s, tc_r = part("ibuf", h), part("tc_s", h), part("tc_r", h)
        tx_s, tx_r = part("tx_s", h), part("tx_r", h)
        wait_all(ibuf.at[rest], s.isem.at[h])

        def table_rows(which):
            return dot(s.hot[block(which, 256), :], ibuf[...].reshape(SLOTS, WIDTHS[h]))

        for dx in FAR_X + (0,):
            tc_s[dx] = table_rows(x_of(dx) * 2 + other).astype(BF16)
            send(tc_s.at[dx], tc_r.at[dx], s.tcs.at[h, dx], s.tcr.at[h, dx], partner)
        for dx in FAR_X + (0,):
            own = table_rows(x_of(dx) * 2 + c)
            wait_all(tc_r.at[dx], s.tcr.at[h, dx])
            own = own + tc_r[dx].astype(F32)
            if dx:
                tx_s[dx] = own.astype(BF16)
                send(tx_s.at[dx], tx_r.at[dx], s.txs.at[h], s.txr.at[h], (t, x_of(dx) * 2 + c))
            else:
                part("tx_own", h)[...] = own

    def table_finish(h):
        tx_r = part("tx_r", h)
        wait_all(tx_r.at[rest_x], s.txr.at[h])
        tgrad_ref[:, STARTS[h] : STARTS[h] + WIDTHS[h]] = (
            part("tx_own", h)[...] + tx_r[1].astype(F32) + tx_r[2].astype(F32) + tx_r[3].astype(F32))

    outer_y()

    for n in range(2):
        out = dot(s.place[...], s.gemb[:, 256 * n : 256 * (n + 1)])
        for h in ((0,), (1, 2))[n]:
            lo = STARTS[h] - 256 * n
            message = out[:, lo : lo + WIDTHS[h]].reshape(NT_DEV, CAP, WIDTHS[h]).astype(BF16)
            obuf, ibuf = part("obuf", h), part("ibuf", h)
            obuf[...] = message
            ibuf[0] = message[0]

            @pl.loop(1, NT_DEV)
            def _(i):
                k = NT_DEV - i
                send(obuf.at[k], ibuf.at[k], s.ssem.at[h], s.isem.at[h], (at_offset(t, k, 1), g))

    inner_core()

    @pl.loop(0, 4)
    def _(r):
        rows = block(r, 128)
        out = dot(s.mixed[rows, :], s.w_out[...])
        res_ref[rows, :] = (s.emb[rows, :].astype(F32) + out).astype(BF16)

    outer_z()
    inner_x()
    table_send(0)
    table_send(1)
    inner_y()
    table_send(2)
    inner_z()
    outer_g()
    table_finish(0)
    table_finish(1)
    wait_all(s.wz_r.at[rest_z], s.wzr.at[0])
    wing_ref[...] = s.wz_own[z] + jnp.sum(s.wz_r[1:].astype(F32), 0)
    wait_all(s.og_r.at[rest_g], s.ogr)
    woutg_ref[...] = jnp.concatenate([s.og_r[lax.rem(g + 2 * NX - k, 2 * NX)] for k in range(2 * NX)], 0)
    table_finish(2)

    wait_all(s.req.at[rest], s.rsend)
    wait_all(s.sbuf.at[rest], s.dsend)
    for h in range(CHUNKS):
        wait_all(part("obuf", h).at[rest], s.ssem.at[h])
        wait_all(part("tx_s", h).at[rest_x], s.txs.at[h])
        for dx in range(NX):
            wait_all(part("tc_s", h).at[dx], s.tcs.at[h, dx])
    for dx in range(NX):
        wait_all(s.wc_s.at[dx], s.wcs.at[dx])
    wait_all(s.oc_r, s.ocs)
    wait_all(s.gx_r.at[rest_g], s.gxs)
    for n, dx in ((0, 1), (1, 3)):
        wait_all(s.wh_s.at[n], s.whs.at[n])
        wait_all(s.wx_s.at[dx], s.wxs.at[dx])
    wait_all(s.ox_s.at[rest_x], s.oxs)
    wait_all(s.wy_s.at[rest_y], s.wys.at[0])
    wait_all(s.oy_s.at[rest_y], s.wys.at[1])
    wait_all(s.gy_r.at[rest_y], s.wys.at[2])
    wait_all(s.wz_s.at[rest_z], s.wzs.at[0])
    wait_all(s.oz_s.at[rest_z], s.wzs.at[1])
    wait_all(s.gz_r.at[rest_z], s.wzs.at[2])
    wait_all(s.og_r.at[rest_g], s.ogs)


def finish_kernel(res, tgrad, wing, woutg, gaing, res_o, tgrad_o, wing_o, woutg_o, gaing_o):
    res_o[...] = res[...]
    tgrad_o[...] = tgrad[...]
    wing_o[...] = wing[...]
    woutg_o[...] = woutg[...]
    gaing_o[...] = gaing[:, :16]


def on_device(item_owner, item_row, lengths, table, w_in, w_out, gain, cotangent):
    vm = pl.BlockSpec(memory_space=pltpu.VMEM)
    hbm = pl.BlockSpec(memory_space=pltpu.HBM)
    shapes = (
        jax.ShapeDtypeStruct((TOK, D), BF16),
        jax.ShapeDtypeStruct((256, D), F32),
        jax.ShapeDtypeStruct((16, 256), F32),
        jax.ShapeDtypeStruct((16, D), F32),
    )
    outs = pl.pallas_call(
        kernel,
        name="whole",
        out_shape=shapes + (jax.ShapeDtypeStruct((1, 128), F32),),
        in_specs=[pl.BlockSpec(memory_space=pltpu.SMEM)] + [hbm] * 7,
        out_specs=[vm] * 5,
        scratch_shapes=list(scratch().values()),
        compiler_params=pltpu.CompilerParams(
            collective_id=1, has_side_effects=True, vmem_limit_bytes=60 * 2**20
        ),
    )(lengths, item_owner.reshape(1, TOK), item_row.reshape(1, TOK), table, w_in, w_out,
      gain.reshape(1, D), cotangent)
    res, tgrad, wing, woutg, gaing = pl.pallas_call(
        finish_kernel,
        name="finish",
        out_shape=shapes + (jax.ShapeDtypeStruct((1, 16), F32),),
        in_specs=[vm] * 5,
        out_specs=[vm] * 5,
    )(*outs)
    return res, tgrad, wing, woutg, gaing.reshape(16)


def solution(mesh):
    return jax.shard_map(
        on_device,
        mesh=mesh,
        in_specs=(
            P(("table", "group"), None),
            P(("table", "group")),
            P(("table", "group"), None),
            P("table", None),
            P(),
            P(),
            P(),
            P(("table", "group"), None),
        ),
        out_specs=(
            P(("table", "group"), None),
            P(("table", "group"), None),
            P("table", "group"),
            P("table", None),
            P("table"),
        ),
        check_vma=False,
    )
```

```python
import types

import jax
import jax.numpy as jnp
from jax import lax
from jax.experimental import pallas as pl
from jax.experimental.pallas import tpu as pltpu
from jax.sharding import PartitionSpec as P

D = 512
TOK = 512
NY, NZ, NX = 4, 8, 4
NT_DEV = NY * NZ
CAP = 24
SLOTS = CAP * NT_DEV
WIDTHS = (256, 128, 128)
STARTS = (0, 256, 384)
CHUNKS = len(WIDTHS)
F32 = jnp.float32
BF16 = jnp.bfloat16
I32 = jnp.int32
NT = (((1,), (1,)), ((), ()))
TN = (((0,), (0,)), ((), ()))
NN = (((1,), (0,)), ((), ()))
MESH = pl.DeviceIdType.MESH
FAR_X = (2, 1, 3)


def dot(a, b, dims=NN):
    return lax.dot_general(a, b, dims, preferred_element_type=F32)


def iota(shape, axis):
    return lax.broadcasted_iota(I32, shape, axis)


def hot(cond):
    return jnp.where(cond, 1.0, 0.0).astype(BF16)


def half_lanes(v, half):
    lane = iota(v.shape, 1)
    keep = (lane < 64) if half == 0 else (lane >= 64)
    return jnp.where(keep, v, jnp.zeros_like(v))


def at_offset(t, k, sign):
    y, z = lax.div(t, NZ), lax.rem(t, NZ)
    step, dy = lax.div(k, NY), lax.rem(k, NY)
    half = lax.div(step + 1, 2)
    dz = jnp.where(lax.rem(step, 2) == 1, half, NZ - half)
    yy = lax.rem(y + sign * dy + NY, NY)
    zz = lax.rem(z + sign * dz + NZ, NZ)
    return yy * NZ + zz


def wait_all(ref, sem):
    pltpu.make_async_copy(ref, ref, sem).wait()


def send(src, dst, send_sem, recv_sem, to):
    pltpu.make_async_remote_copy(
        src_ref=src, dst_ref=dst, send_sem=send_sem, recv_sem=recv_sem,
        device_id=to, device_id_type=MESH,
    ).start()


def block(i, size):
    return pl.ds(pl.multiple_of(i * size, size), size)


def scratch():
    vm = pltpu.VMEM
    dma = pltpu.SemaphoreType.DMA
    return dict(
        own=vm((1, TOK), I32), row=vm((1, TOK), I32), table=vm((2048, D), BF16),
        w_in=vm((D, 2048), BF16), w_out=vm((D, D), BF16), cot=vm((TOK, D), BF16),
        gain=vm((1, D), F32),
        req=vm((NT_DEV, 1, 128), I32), got=vm((NT_DEV, 1, 128), I32),
        onehot=vm((24 * NZ, 2048), BF16), sbuf=vm((NT_DEV, CAP, D), BF16),
        rbuf=vm((NT_DEV, CAP, D), BF16), place=vm((SLOTS, TOK), BF16),
        hot=vm((2048, SLOTS), BF16),
        emb=vm((TOK, D), BF16), emb_t=vm((D, TOK), BF16), w_in_t=vm((2048, D), BF16),
        slope=vm((TOK, 2048), F32), proj=vm((TOK, 2048), BF16), w=vm((8, TOK, TOK), BF16),
        d=vm((8, TOK, TOK), F32), mask=vm((TOK, TOK), F32), att=vm((TOK, D), F32),
        gmix=vm((TOK, D), F32), gatt=vm((TOK, D), BF16), gpre=vm((TOK, 2048), BF16),
        mixed=vm((TOK, D), BF16), gacc=vm((2, 256, 128), F32), gemb=vm((TOK, D), BF16),
        order=vm((D, D), BF16), gwout=vm((D, D), BF16), ggain=vm((1, D), F32),
        **{f"obuf{h}": vm((NT_DEV, CAP, w), BF16) for h, w in enumerate(WIDTHS)},
        **{f"ibuf{h}": vm((NT_DEV, CAP, w), BF16) for h, w in enumerate(WIDTHS)},
        **{f"{n}{h}": vm((NX, 256, w), BF16) for h, w in enumerate(WIDTHS)
           for n in ("tc_s", "tc_r", "tx_s", "tx_r")},
        **{f"tx_own{h}": vm((256, w), F32) for h, w in enumerate(WIDTHS)},
        wc_s=vm((NX, D, 256), BF16), wc_r=vm((NX, D, 256), BF16), oc_r=vm((NX, 64, D), BF16),
        wx_s=vm((NX, D, 256), BF16), wx_r=vm((NX, D, 256), BF16), wf=vm((NX, D, 256), F32), wh_s=vm((2, 256, 256), BF16), wh_r=vm((2, 256, 256), BF16),
        ox_s=vm((NX, 64, D), BF16), ox_r=vm((NX, 64, D), BF16), ox_own=vm((64, D), F32),
        gx_r=vm((2 * NX, 1, D), F32),
        wy_s=vm((NY, 128, 256), BF16), wy_r=vm((NY, 128, 256), BF16), wy_own=vm((NY, 128, 256), F32),
        oy_s=vm((NY, 16, D), BF16), oy_r=vm((NY, 16, D), BF16), oy_own=vm((NY, 16, D), F32),
        gy_s=vm((1, D), F32), gy_r=vm((NY, 1, D), F32),
        wz_s=vm((NZ, 16, 256), BF16), wz_r=vm((NZ, 16, 256), BF16), wz_own=vm((NZ, 16, 256), F32),
        oz_s=vm((NZ, 2, D), F32), oz_r=vm((NZ, 2, D), F32),
        gz_s=vm((1, D), F32), gz_r=vm((NZ, 1, D), F32),
        og_s=vm((2, D), F32), og_r=vm((2 * NX, 2, D), F32),
        load=dma((7,)), rsend=dma, rrecv=dma((NY,)), dsend=dma, drecv=dma,
        ssem=dma((CHUNKS,)), isem=dma((CHUNKS,)),
        tcs=dma((CHUNKS, NX)), tcr=dma((CHUNKS, NX)), txs=dma((CHUNKS,)), txr=dma((CHUNKS,)),
        wcs=dma((NX,)), wcr=dma((NX,)), ocs=dma, ocr=dma, gxs=dma, gxr=dma,
        wxs=dma((NX,)), wxr=dma((NX,)), whs=dma((2,)), whr=dma((2,)), oxs=dma, oxr=dma, wys=dma((3,)), wyr=dma((3,)), wzs=dma((3,)), wzr=dma((3,)),
        ogs=dma, ogr=dma,
    )


def kernel(len_ref, own_h, row_h, table_h, w_in_h, w_out_h, gain_h, cot_h,
           res_ref, tgrad_ref, wing_ref, woutg_ref, gaing_ref, *refs):
    s = types.SimpleNamespace(**dict(zip(scratch(), refs)))

    def part(name, h):
        return getattr(s, name + str(h))

    t, g = lax.axis_index("table"), lax.axis_index("group")
    x, c = lax.div(g, 2), lax.rem(g, 2)
    other = 1 - c
    y, z = lax.div(t, NZ), lax.rem(t, NZ)
    partner = (t, x * 2 + other)
    barrier = pltpu.get_barrier_semaphore()

    loads = [
        pltpu.make_async_copy(src, dst, s.load.at[i])
        for i, (src, dst) in enumerate((
            (own_h, s.own), (row_h, s.row), (table_h, s.table), (w_out_h, s.w_out),
            (cot_h, s.cot), (w_in_h, s.w_in), (gain_h, s.gain)))
    ]
    for copy in loads:
        copy.start()

    @pl.loop(1, NT_DEV)
    def _(k):
        pl.semaphore_signal(
            barrier, inc=1, device_id=(at_offset(t, NT_DEV - k, 1), g), device_id_type=MESH)

    @pl.loop(1, 2 * NX)
    def _(k):
        pl.semaphore_signal(
            barrier, inc=1, device_id=(t, lax.rem(g + k, 2 * NX)), device_id_type=MESH)

    def x_of(dx):
        return lax.rem(x + dx, NX)

    loads[0].wait()
    loads[1].wait()
    own = s.own[...]
    dy = (lax.shift_right_logical(own, 3) - y) & (NY - 1)
    dz = ((own & (NZ - 1)) - z) & (NZ - 1)
    step = jnp.where(dz == 0, 0, jnp.where(dz <= NZ // 2, 2 * dz - 1, 2 * (NZ - dz)))
    rel = step * NY + dy
    is_rel = rel == iota((NT_DEV, TOK), 0)
    before = dot(hot(is_rel), hot(iota((TOK, TOK), 0) < iota((TOK, TOK), 1)))
    rank = jnp.sum(jnp.where(is_rel, before, 0.0), 0, keepdims=True).astype(I32)
    idx = s.row[...] + 1
    ranks = hot(rank == iota((128, TOK), 0))
    high = jnp.where(is_rel, lax.shift_right_logical(idx, 6).astype(F32), 0.0).astype(BF16)
    low = jnp.where(is_rel, (idx & 63).astype(F32), 0.0).astype(BF16)
    wanted = dot(high, ranks, NT) * 64.0 + dot(low, ranks, NT)
    s.req[...] = wanted.astype(I32).reshape(NT_DEV, 1, 128)
    s.got[0] = s.req[0]

    pl.semaphore_wait(barrier, NT_DEV - 1 + 2 * NX - 1)

    @pl.loop(1, NT_DEV)
    def _(i):
        k = NT_DEV - i
        send(s.req.at[k], s.got.at[k], s.rsend, s.rrecv.at[lax.div(k, 8)], (at_offset(t, k, 1), g))

    s.place[...] = hot(rel * CAP + rank == iota((SLOTS, TOK), 0))
    loads[2].wait()

    for b in range(4):
        first = 1 if b == 0 else 0
        wait_all(s.got.at[pl.ds(NZ * b + first, NZ - first)], s.rrecv.at[b])
        names = jnp.transpose(s.got[NZ * b : NZ * (b + 1), 0, :].astype(F32))
        col = jnp.concatenate(
            [names[:CAP, j : j + 1] for j in range(NZ)], 0).astype(I32)
        for q in range(4):
            s.onehot[:, 512 * q : 512 * (q + 1)] = hot(col == 512 * q + 1 + iota((24 * NZ, 512), 1))
        rows = dot(s.onehot[...], s.table[...])
        message = rows.reshape(NZ, CAP, D).astype(BF16)
        s.sbuf[NZ * b : NZ * (b + 1)] = message
        if b == 0:
            s.rbuf[0] = message[0]

        @pl.loop(first, NZ)
        def _(i):
            k = NZ * b + (NZ - 1 + first - i)
            send(s.sbuf.at[k], s.rbuf.at[k], s.dsend, s.drecv, (at_offset(t, k, -1), g))

    ids = s.got[:, 0, :]
    high = lax.shift_right_logical(ids, 6).astype(F32).astype(BF16)
    low = (ids & 63).astype(F32).astype(BF16)

    lane = iota((NT_DEV, SLOTS), 1)
    source = jnp.floor((lane.astype(F32) + 0.5) * (1.0 / CAP)).astype(I32)
    lane = iota((128, SLOTS), 1)
    turn = lane - CAP * jnp.floor((lane.astype(F32) + 0.5) * (1.0 / CAP)).astype(I32)
    pick = hot(iota((128, SLOTS), 0) == turn)
    both = dot(high, pick) * 64.0 + dot(low, pick)
    mine = iota((NT_DEV, SLOTS), 0) == source
    name = jnp.sum(jnp.where(mine, both, 0.0), 0, keepdims=True).astype(I32)

    @pl.loop(0, 8)
    def _(i):
        s.hot[block(i, 256), :] = hot(name == i * 256 + 1 + iota((256, SLOTS), 0))

    ends = []
    total = jnp.int32(0)
    for k in range(8):
        total = total + len_ref[0, k]
        ends.append(total)
    for r in range(4):
        pos = 128 * r + iota((128, 128), 0)
        start = jnp.zeros((128, 128), I32)
        for e in ends:
            start = jnp.where(pos >= e, e, start)
        for q in range(4):
            col = 128 * q + iota((128, 128), 1)
            ok = (col >= start) & (col <= pos)
            s.mask[128 * r : 128 * (r + 1), 128 * q : 128 * (q + 1)] = jnp.where(ok, 1.0, 0.0)

    loads[3].wait()
    loads[4].wait()

    @pl.loop(0, 4)
    def _(r):
        rows = block(r, 128)
        s.gmix[rows, :] = dot(s.cot[rows, :], s.w_out[...], NT).astype(BF16).astype(F32)

    lane = iota((D, D), 1)
    source = ((lane >> 1) & 31) * 16 + (lane >> 6) * 2 + (lane & 1)
    s.order[...] = hot(iota((D, D), 0) == source)
    loads[5].wait()
    loads[6].wait()

    @pl.loop(0, 8)
    def _(q):
        s.w_in_t[block(q, 256), :] = jnp.transpose(s.w_in[:, block(q, 256)])

    rest = pl.ds(1, NT_DEV - 1)
    wait_all(s.rbuf.at[rest], s.drecv)
    s.emb[...] = dot(s.place[...], s.rbuf[...].reshape(SLOTS, D), TN).astype(BF16)

    @pl.loop(0, 8, unroll=4)
    def _(q):
        cols = block(q, 256)
        pre = dot(s.emb[...], s.w_in[:, cols])
        sig = 0.5 + 0.5 * jnp.tanh(0.5 * pre)
        act = pre * sig
        s.proj[:, cols] = act.astype(BF16)
        s.slope[:, cols] = sig + act * (1.0 - sig)

    @pl.loop(0, 4, unroll=4)
    def _(p):
        off = pl.multiple_of(p * 128, 128)
        for r in range(2):
            rows = pl.ds(256 * r, 256)
            cols = pl.ds(0, 256 * (r + 1))
            key = s.proj[cols, pl.ds(1536 + off, 128)]
            val = s.proj[cols, pl.ds(512 + off, 128)]
            qry = s.proj[rows, pl.ds(1024 + off, 128)] * jnp.asarray(0.0625, BF16)
            mask = s.mask[rows, cols]
            acc = None
            for half in range(2):
                h = dot(half_lanes(qry, half), key, NT)
                th = jnp.tanh(h)
                um = (1.0 + th) * mask
                w = h * um
                s.d[2 * p + half, rows, cols] = um + w * (1.0 - th)
                wb = w.astype(BF16)
                s.w[2 * p + half, rows, cols] = wb
                some = dot(wb, half_lanes(val, half))
                acc = some if acc is None else acc + some
            s.att[rows, pl.ds(off, 128)] = acc

    s.ggain[...] = jnp.zeros_like(s.ggain)

    @pl.loop(0, 4, unroll=2)
    def _(r):
        rows = block(r, 128)
        att = s.att[rows, :]
        cen = att - jnp.mean(att, 1, keepdims=True)
        inv = lax.rsqrt(jnp.mean(cen * cen, 1, keepdims=True) + 1e-05)
        normed = cen * inv
        gain = s.gain[...]
        upd = s.proj[rows, pl.ds(0, 512)].astype(F32)
        s.mixed[rows, :] = (normed * gain * upd).astype(BF16)
        gmix = s.gmix[rows, :]
        gn = gmix * normed
        s.gpre[rows, pl.ds(0, 512)] = (gn * gain * s.slope[rows, pl.ds(0, 512)]).astype(BF16)
        s.ggain[...] += jnp.sum(gn * upd, 0, keepdims=True)
        gnorm = gmix * gain * upd
        m1 = jnp.mean(gnorm, 1, keepdims=True)
        m2 = jnp.mean(gnorm * normed, 1, keepdims=True)
        s.gatt[rows, :] = ((gnorm - m1 - normed * m2) * inv).astype(BF16)

    mixed = dot(s.mixed[...], s.order[...]).astype(BF16)
    s.gwout[...] = dot(mixed, s.cot[...], TN).astype(BF16)
    s.gx_r[0] = s.ggain[...]

    @pl.loop(0, NX)
    def _(dx):
        send(s.gwout.at[block(x_of(dx) * 2 + other, 64), :], s.oc_r.at[dx], s.ocs, s.ocr, partner)

    @pl.loop(1, 2 * NX)
    def _(k):
        send(s.ggain, s.gx_r.at[k], s.gxs, s.gxr, (t, lax.rem(g + k, 2 * NX)))

    def back_pair(p):
        off = pl.multiple_of(p * 128, 128)
        for r in range(2):
            rows = pl.ds(256 * r, 256)
            cols = pl.ds(0, 256 * (r + 1))
            key = s.proj[cols, pl.ds(1536 + off, 128)] * jnp.asarray(0.0625, BF16)
            val = s.proj[cols, pl.ds(512 + off, 128)]
            qry = s.proj[rows, pl.ds(1024 + off, 128)] * jnp.asarray(0.0625, BF16)
            gat = s.gatt[rows, pl.ds(off, 128)]
            gq = gk = gv = None
            for half in range(2):
                gath = half_lanes(gat, half)
                gw = dot(gath, val, NT)
                gs = (gw * s.d[2 * p + half, rows, cols]).astype(BF16)
                a = dot(gs, half_lanes(key, half))
                b = dot(gs, half_lanes(qry, half), TN)
                v = dot(s.w[2 * p + half, rows, cols], gath, TN)
                gq = a if gq is None else gq + a
                gk = b if gk is None else gk + b
                gv = v if gv is None else gv + v
            qcols = pl.ds(1024 + off, 128)
            s.gpre[rows, qcols] = (gq * s.slope[rows, qcols]).astype(BF16)
            if r == 0:
                s.gacc[0] = gk
                s.gacc[1] = gv
            else:
                for n, acc in ((0, gk), (1, gv)):
                    dst = pl.ds((1536 if n == 0 else 512) + off, 128)
                    for half in range(2):
                        here = pl.ds(256 * half, 256)
                        v = acc[256 * half : 256 * (half + 1)]
                        v = v + s.gacc[n] if half == 0 else v
                        s.gpre[here, dst] = (v * s.slope[here, dst]).astype(BF16)

    pl.loop(0, 2, unroll=2)(back_pair)
    wait_all(s.oc_r, s.ocr)
    for dx in FAR_X + (0,):
        o = s.gwout[block(x_of(dx) * 2 + c, 64), :].astype(F32) + s.oc_r[dx].astype(F32)
        if dx:
            s.ox_s[dx] = o.astype(BF16)
            send(s.ox_s.at[dx], s.ox_r.at[dx], s.oxs, s.oxr, (t, x_of(dx) * 2 + c))
        else:
            s.ox_own[...] = o
    pl.loop(2, 4, unroll=2)(back_pair)

    @pl.loop(0, 2, unroll=2)
    def _(q):
        cols = block(q, 256)
        v = dot(s.gpre[...], s.w_in_t[:, cols])
        s.gemb[:, cols] = (s.cot[:, cols].astype(F32) + v).astype(BF16)

    rest_x, rest_y, rest_z = pl.ds(1, NX - 1), pl.ds(1, NY - 1), pl.ds(1, NZ - 1)
    rest_g = pl.ds(1, 2 * NX - 1)

    def outer_y():
        wait_all(s.ox_r.at[rest_x], s.oxr)
        wait_all(s.gx_r.at[rest_g], s.gxr)
        o = s.ox_own[...] + s.ox_r[1].astype(F32) + s.ox_r[2].astype(F32) + s.ox_r[3].astype(F32)
        s.oy_own[...] = o.reshape(NY, 16, D)
        s.oy_s[...] = o.astype(BF16).reshape(NY, 16, D)
        s.gy_s[...] = jnp.sum(s.gx_r[...], 0)
        s.gy_r[0] = s.gy_s[...]

        @pl.loop(1, NY)
        def _(k):
            yy = lax.rem(y + k, NY)
            to = (yy * NZ + z, g)
            send(s.oy_s.at[yy], s.oy_r.at[k], s.wys.at[1], s.wyr.at[1], to)
            send(s.gy_s, s.gy_r.at[k], s.wys.at[2], s.wyr.at[2], to)

    def outer_z():
        wait_all(s.oy_r.at[rest_y], s.wyr.at[1])
        wait_all(s.gy_r.at[rest_y], s.wyr.at[2])
        o = s.oy_own[y] + s.oy_r[1].astype(F32) + s.oy_r[2].astype(F32) + s.oy_r[3].astype(F32)
        for k in range(NZ):
            s.oz_s[k] = o[2 * k : 2 * k + 2]
        s.gz_s[...] = jnp.sum(s.gy_r[...], 0)
        s.gz_r[0] = s.gz_s[...]
        s.oz_r[0] = s.oz_s[z]

        @pl.loop(1, NZ)
        def _(k):
            zz = lax.rem(z + k, NZ)
            to = (y * NZ + zz, g)
            send(s.oz_s.at[zz], s.oz_r.at[k], s.wzs.at[1], s.wzr.at[1], to)
            send(s.gz_s, s.gz_r.at[k], s.wzs.at[2], s.wzr.at[2], to)

    def outer_g():
        wait_all(s.oz_r.at[rest_z], s.wzr.at[1])
        s.og_s[...] = jnp.sum(s.oz_r[...], 0)
        s.og_r[0] = s.og_s[...]

        @pl.loop(1, 2 * NX)
        def _(k):
            send(s.og_s, s.og_r.at[k], s.ogs, s.ogr, (t, lax.rem(g + k, 2 * NX)))

    def gain_finish():
        wait_all(s.gz_r.at[rest_z], s.wzr.at[2])
        total = jnp.sum(s.gz_r[...], 0)
        pick = jnp.where(iota((D, 128), 0) == 16 * t + iota((D, 128), 1), 1.0, 0.0)
        gaing_ref[...] = lax.dot_general(
            jnp.broadcast_to(total, (8, D)), pick, NN,
            precision=lax.Precision.HIGHEST, preferred_element_type=F32)[:1]

    def inner_core():
        s.emb_t[...] = jnp.transpose(s.emb[...])
        for dx in FAR_X + (0,):
            cols = block(x_of(dx) * 2 + other, 256)
            s.wc_s[dx] = dot(s.emb_t[...], s.gpre[:, cols]).astype(BF16)
            send(s.wc_s.at[dx], s.wc_r.at[dx], s.wcs.at[dx], s.wcr.at[dx], partner)
        for dx in FAR_X + (0,):
            w = dot(s.emb_t[...], s.gpre[:, block(x_of(dx) * 2 + c, 256)])
            wait_all(s.wc_r.at[dx], s.wcr.at[dx])
            w = w + s.wc_r[dx].astype(F32)
            if dx == 2:
                for n, to in ((0, 1), (1, 3)):
                    s.wh_s[n] = w[256 * n : 256 * (n + 1)].astype(BF16)
                    send(s.wh_s.at[n], s.wh_r.at[n], s.whs.at[n], s.whr.at[n],
                         (t, x_of(to) * 2 + c))
            else:
                s.wf[dx] = w

    def inner_x():
        for n, dx in ((0, 1), (1, 3)):
            wait_all(s.wh_r.at[n], s.whr.at[n])
            near, far = pl.ds(256 * n, 256), pl.ds(256 * (1 - n), 256)
            s.wx_s[dx, near, :] = (s.wf[dx, near, :] + s.wh_r[n].astype(F32)).astype(BF16)
            s.wx_s[dx, far, :] = s.wf[dx, far, :].astype(BF16)
            send(s.wx_s.at[dx], s.wx_r.at[dx], s.wxs.at[dx], s.wxr.at[dx], (t, x_of(dx) * 2 + c))

    def inner_y():
        wait_all(s.wx_r.at[1], s.wxr.at[1])
        wait_all(s.wx_r.at[3], s.wxr.at[3])
        w = s.wf[0] + s.wx_r[1].astype(F32) + s.wx_r[3].astype(F32)
        s.wy_own[...] = w.reshape(NY, 128, 256)
        s.wy_s[...] = w.astype(BF16).reshape(NY, 128, 256)

        @pl.loop(1, NY)
        def _(k):
            yy = lax.rem(y + k, NY)
            send(s.wy_s.at[yy], s.wy_r.at[k], s.wys.at[0], s.wyr.at[0], (yy * NZ + z, g))

    def inner_z():
        wait_all(s.wy_r.at[rest_y], s.wyr.at[0])
        w = s.wy_own[y] + s.wy_r[1].astype(F32) + s.wy_r[2].astype(F32) + s.wy_r[3].astype(F32)
        s.wz_own[...] = w.reshape(NZ, 16, 256)
        s.wz_s[...] = w.astype(BF16).reshape(NZ, 16, 256)

        @pl.loop(1, NZ)
        def _(k):
            zz = lax.rem(z + k, NZ)
            send(s.wz_s.at[zz], s.wz_r.at[k], s.wzs.at[0], s.wzr.at[0], (y * NZ + zz, g))

    def table_send(h):
        ibuf, tc_s, tc_r = part("ibuf", h), part("tc_s", h), part("tc_r", h)
        tx_s, tx_r = part("tx_s", h), part("tx_r", h)
        wait_all(ibuf.at[rest], s.isem.at[h])

        def table_rows(which):
            return dot(s.hot[block(which, 256), :], ibuf[...].reshape(SLOTS, WIDTHS[h]))

        for dx in FAR_X + (0,):
            tc_s[dx] = table_rows(x_of(dx) * 2 + other).astype(BF16)
            send(tc_s.at[dx], tc_r.at[dx], s.tcs.at[h, dx], s.tcr.at[h, dx], partner)
        for dx in FAR_X + (0,):
            own = table_rows(x_of(dx) * 2 + c)
            wait_all(tc_r.at[dx], s.tcr.at[h, dx])
            own = own + tc_r[dx].astype(F32)
            if dx:
                tx_s[dx] = own.astype(BF16)
                send(tx_s.at[dx], tx_r.at[dx], s.txs.at[h], s.txr.at[h], (t, x_of(dx) * 2 + c))
            else:
                part("tx_own", h)[...] = own

    def table_finish(h):
        tx_r = part("tx_r", h)
        wait_all(tx_r.at[rest_x], s.txr.at[h])
        tgrad_ref[:, STARTS[h] : STARTS[h] + WIDTHS[h]] = (
            part("tx_own", h)[...] + tx_r[1].astype(F32) + tx_r[2].astype(F32) + tx_r[3].astype(F32))

    outer_y()

    for n in range(2):
        out = dot(s.place[...], s.gemb[:, 256 * n : 256 * (n + 1)])
        for h in ((0,), (1, 2))[n]:
            lo = STARTS[h] - 256 * n
            message = out[:, lo : lo + WIDTHS[h]].reshape(NT_DEV, CAP, WIDTHS[h]).astype(BF16)
            obuf, ibuf = part("obuf", h), part("ibuf", h)
            obuf[...] = message
            ibuf[0] = message[0]

            @pl.loop(1, NT_DEV)
            def _(i):
                k = NT_DEV - i
                send(obuf.at[k], ibuf.at[k], s.ssem.at[h], s.isem.at[h], (at_offset(t, k, 1), g))

    inner_core()

    @pl.loop(0, 4)
    def _(r):
        rows = block(r, 128)
        out = dot(s.mixed[rows, :], s.w_out[...])
        res_ref[rows, :] = (s.emb[rows, :].astype(F32) + out).astype(BF16)

    outer_z()
    inner_x()
    table_send(0)
    table_send(1)
    inner_y()
    table_send(2)
    outer_g()
    inner_z()
    gain_finish()
    table_finish(0)
    table_finish(1)
    wait_all(s.wz_r.at[rest_z], s.wzr.at[0])
    wing_ref[...] = s.wz_own[z] + jnp.sum(s.wz_r[1:].astype(F32), 0)
    wait_all(s.og_r.at[rest_g], s.ogr)
    woutg_ref[...] = jnp.concatenate([s.og_r[lax.rem(g + 2 * NX - k, 2 * NX)] for k in range(2 * NX)], 0)
    table_finish(2)

    wait_all(s.req.at[rest], s.rsend)
    wait_all(s.sbuf.at[rest], s.dsend)
    for h in range(CHUNKS):
        wait_all(part("obuf", h).at[rest], s.ssem.at[h])
        wait_all(part("tx_s", h).at[rest_x], s.txs.at[h])
        for dx in range(NX):
            wait_all(part("tc_s", h).at[dx], s.tcs.at[h, dx])
    for dx in range(NX):
        wait_all(s.wc_s.at[dx], s.wcs.at[dx])
    wait_all(s.oc_r, s.ocs)
    wait_all(s.gx_r.at[rest_g], s.gxs)
    for n, dx in ((0, 1), (1, 3)):
        wait_all(s.wh_s.at[n], s.whs.at[n])
        wait_all(s.wx_s.at[dx], s.wxs.at[dx])
    wait_all(s.ox_s.at[rest_x], s.oxs)
    wait_all(s.wy_s.at[rest_y], s.wys.at[0])
    wait_all(s.oy_s.at[rest_y], s.wys.at[1])
    wait_all(s.gy_r.at[rest_y], s.wys.at[2])
    wait_all(s.wz_s.at[rest_z], s.wzs.at[0])
    wait_all(s.oz_s.at[rest_z], s.wzs.at[1])
    wait_all(s.gz_r.at[rest_z], s.wzs.at[2])
    wait_all(s.og_r.at[rest_g], s.ogs)


def finish_kernel(res, tgrad, wing, woutg, gaing, res_o, tgrad_o, wing_o, woutg_o, gaing_o):
    res_o[...] = res[...]
    tgrad_o[...] = tgrad[...]
    wing_o[...] = wing[...]
    woutg_o[...] = woutg[...]
    gaing_o[...] = gaing[:, :16]


def on_device(item_owner, item_row, lengths, table, w_in, w_out, gain, cotangent):
    vm = pl.BlockSpec(memory_space=pltpu.VMEM)
    hbm = pl.BlockSpec(memory_space=pltpu.HBM)
    shapes = (
        jax.ShapeDtypeStruct((TOK, D), BF16),
        jax.ShapeDtypeStruct((256, D), F32),
        jax.ShapeDtypeStruct((16, 256), F32),
        jax.ShapeDtypeStruct((16, D), F32),
    )
    outs = pl.pallas_call(
        kernel,
        name="whole",
        out_shape=shapes + (jax.ShapeDtypeStruct((1, 128), F32),),
        in_specs=[pl.BlockSpec(memory_space=pltpu.SMEM)] + [hbm] * 7,
        out_specs=[vm] * 5,
        scratch_shapes=list(scratch().values()),
        compiler_params=pltpu.CompilerParams(
            collective_id=1, has_side_effects=True, vmem_limit_bytes=60 * 2**20
        ),
    )(lengths, item_owner.reshape(1, TOK), item_row.reshape(1, TOK), table, w_in, w_out,
      gain.reshape(1, D), cotangent)
    res, tgrad, wing, woutg, gaing = pl.pallas_call(
        finish_kernel,
        name="finish",
        out_shape=shapes + (jax.ShapeDtypeStruct((1, 16), F32),),
        in_specs=[vm] * 5,
        out_specs=[vm] * 5,
    )(*outs)
    return res, tgrad, wing, woutg, gaing.reshape(16)


def solution(mesh):
    return jax.shard_map(
        on_device,
        mesh=mesh,
        in_specs=(
            P(("table", "group"), None),
            P(("table", "group")),
            P(("table", "group"), None),
            P("table", None),
            P(),
            P(),
            P(),
            P(("table", "group"), None),
        ),
        out_specs=(
            P(("table", "group"), None),
            P(("table", "group"), None),
            P("table", "group"),
            P("table", None),
            P("table"),
        ),
        check_vma=False,
    )
```
